128 devices in a mesh: ref: 16 (over y, x_hi, core), img: 8 (over x_lo, z).
Axes of the slice: x: 4 (x_hi: 2, x_lo: 2; x = x_hi * 2 + x_lo), y: 4, z: 4, core: 2. Of those that a mesh axis runs over, the one named last changes fastest.
Arguments:
- images: bfloat16 [16384, 4096], P(('img', 'ref')), may hold values from -6 to 6
- exponents: int32 [16384], P('img'), may hold values from 0 to 8
- references: bfloat16 [12288, 4096], P('ref'), may hold values from -8 to 8
- partners: int32 [12288], P('ref'), may hold values from 0 to 12287, as said below
Outputs:
- symmetric_sums: float32 [12288, 4096], P('ref', 'img')
The draws below stay inside these ranges and needn't reach their ends.
Inputs may be any that keep to these rules, and one draw needn't show every extreme that they name: partners is an involution without fixed points; partners[r] lies in the block of 768 references that starts 12288 / 2 references after or before the start of r's block.
All inputs are finite; a program needn't handle non-finite values.
Results may differ from the reference program's by a relative error of at most 0.0033.
Values may be sent and summed in bfloat16 or wider, within the bound.
A program may use at most 64 MiB of HBM per device.

```python
import jax
import jax.numpy as jnp
from jax import lax

K = 4096
REF_DEV = 768
NREF = 12288
NIMG = 16384


def draw_references(key, part):
    scale_key = jax.random.fold_in(key, 11)
    value_key = jax.random.fold_in(key, 12)
    scales = jnp.exp(jax.random.uniform(scale_key, (NREF, 1), jnp.float32, jnp.log(0.5), jnp.log(1.5)))
    values = jnp.clip(jax.random.normal(value_key, (NREF, K), jnp.float32), -5.0, 5.0)
    return (values * scales).astype(jnp.bfloat16)


def draw_partners(key, part):
    pair_count = NREF // REF_DEV // 2
    keys = jax.random.split(jax.random.fold_in(key, 21), pair_count)
    perms = jax.vmap(lambda k: jax.random.permutation(k, REF_DEV))(keys).astype(jnp.int32)
    lower = jnp.arange(NREF // 2, dtype=jnp.int32)
    blocks = lower // REF_DEV
    local = lower % REF_DEV
    upper = (NREF // 2 + blocks * REF_DEV + perms[blocks, local]).astype(jnp.int32)
    result = jnp.zeros((NREF,), jnp.int32)
    result = result.at[lower].set(upper)
    result = result.at[upper].set(lower)
    return result


def with_ends(drawn, rng, smallest, high):
    longest = drawn.shape.index(max(drawn.shape))
    spots = []
    for shift in (0, 1):
        where = [jax.random.randint(jax.random.fold_in(rng, axis), (), 0, length) for axis, length in enumerate(drawn.shape)]
        where[longest] = (where[longest] + shift) % drawn.shape[longest]
        spots.append(tuple(where))
    return drawn.at[spots[0]].set(smallest).at[spots[1]].set(high)


def block_scale(key, shape, cuts, smallest, top_value):
    loudness = 1.0
    for axis_at, blocks in cuts:
        steps = jax.random.uniform(jax.random.fold_in(jax.random.fold_in(key, 6), axis_at), (blocks,), jnp.float32, smallest / len(cuts), top_value / len(cuts))
        loudness = loudness * jnp.repeat(jnp.exp(steps), shape[axis_at] // blocks).reshape((-1,) + (1,) * (len(shape) - 1 - axis_at))
    return loudness


def noise(own_key, shape, spread, bound, pieces=(), kind=jnp.bfloat16):
    factor_of = block_scale(own_key, shape, pieces, -0.22, 0.18) if pieces else 1.0
    array = jax.random.normal(own_key, shape, jnp.float32) * spread * factor_of
    return jnp.minimum(jnp.maximum(array, -bound), bound).astype(kind)


def setup_inputs(seed: int = 0) -> dict:
    streams_of = jax.random.split(jax.random.key(seed), 5)
    return {
        "images": noise(streams_of[0], (NIMG, K), 1.0, 6.0, ((0, 128),)),
        "exponents": with_ends(jax.random.randint(streams_of[1], (NIMG,), 0, 9), jax.random.fold_in(streams_of[1], 1), 0, 8).astype(jnp.int32),
        "references": draw_references(jax.random.fold_in(streams_of[4], 71), 0),
        "partners": draw_partners(jax.random.fold_in(streams_of[4], 71), 0),
    }


def reference(images, exponents, references, partners):
    width = references.shape[1]
    norms = lax.optimization_barrier(jnp.sum(jnp.square(references.astype(jnp.float32)), axis=1)) / width
    block = min(512, NIMG)
    count = NIMG // block
    image_blocks = images.reshape(count, block, width)
    expo_blocks = exponents.reshape(count, block)

    def accumulate(total, pair):
        rows, expo = pair
        scores = jnp.dot(rows, references.T, preferred_element_type=jnp.float32) / jnp.sqrt(jnp.float32(width))
        scores = scores - 0.5 * norms[None, :] - 0.25 * expo.astype(jnp.float32)[:, None]
        weights = jnp.exp(scores).astype(jnp.bfloat16)
        return (total + jnp.dot(weights.T, rows, preferred_element_type=jnp.float32), None)
    start = jnp.zeros((references.shape[0], width), jnp.float32)
    sums, _ = lax.scan(accumulate, start, (image_blocks, expo_blocks))
    partner_rows = jnp.take(sums, partners.astype(jnp.int32), axis=0)
    return 0.5 * (sums + partner_rows) / jnp.sqrt(jnp.float32(NIMG))
```

```python
import jax
import jax.numpy as jnp
from jax import lax
from jax.experimental import pallas as pl
from jax.experimental.pallas import tpu as pltpu
from jax.sharding import PartitionSpec as P

MESH = pl.DeviceIdType.MESH
F32 = jnp.float32
BF16 = jnp.bfloat16

R = 768
K = 4096
W = 512
ROWS = 128
UNIT = 256
CUT = 80
RA = 432
RB = R - RA
HALF = W // 2

SLOT = {(0, 0): 0, (0, 1): 1, (0, -1): 2, (1, 0): 3, (1, 1): 4, (1, -1): 5, (0, 2): 6, (1, 2): 7}
ORDER = [dy for _ in range(1) for dy in (2, 1, 3, 0)]


def kernel(images, expo, refs_hbm, partners, out, img, refs, acc, wts, norms, pick, expo_x,
           st_a, st_a2, st_a3, st_b1, st_b2, st_b3, st_b3d, r_a1, r_a2, r_a3, r_b1, r_b2, r_b3,
           final, relay, other, local_sem, send_sem, recv_sem):
    ref, im = lax.axis_index("ref"), lax.axis_index("img")
    y, h, c = ref // 4, (ref // 2) % 2, ref % 2
    l, z = im // 4, im % 4

    def device(y, h, c, l, z):
        return {"ref": y * 4 + h * 2 + c, "img": l * 4 + z}

    up = device((y + 1) % 4, h, c, l, z)
    down = device((y + 3) % 4, h, c, l, z)
    across = device(y, 1 - h, c, 1 - l, z)
    sibling = device(y, h, 1 - c, l, z)
    beside = device(y, h, c, 1 - l, z)
    above = device(y, h, c, l, (z + 1) % 4)
    below = device(y, h, c, l, (z + 3) % 4)

    get_refs = pltpu.make_async_copy(refs_hbm, refs, local_sem.at[0])
    get_refs.start()
    own_rows = pl.ds(pl.multiple_of(c * ROWS, ROWS), ROWS)
    get_own = pltpu.make_async_copy(images, img.at[own_rows, :], local_sem.at[1])
    get_own.start()

    neighbours = (up, down, across, sibling, beside, above, below)
    barrier = pltpu.get_barrier_semaphore()
    for who in neighbours:
        pl.semaphore_signal(barrier, inc=1, device_id=who, device_id_type=MESH)
    pl.semaphore_wait(barrier, len(neighbours))

    copies = {}

    def send(name, src, dst, who):
        at = len(copies)
        copies[name] = pltpu.make_async_remote_copy(
            src_ref=src, dst_ref=dst, send_sem=send_sem.at[at], recv_sem=recv_sem.at[at],
            device_id=who, device_id_type=MESH)
        copies[name].start()

    def arrived(*names):
        for name in names:
            copies[name].wait_recv()

    def part(slot, first=0, count=ROWS, columns=slice(0, K)):
        return img.at[pl.ds(pl.multiple_of(slot * UNIT + c * ROWS + first, 16), count), columns]

    left, right = slice(0, K // 2), slice(K // 2, K)
    a_rows, b_rows = (0, CUT), (CUT, ROWS - CUT)

    send("expo", expo, expo_x, across)
    send("up_own", images, part(SLOT[0, -1]), up)
    send("down_own", images, part(SLOT[0, 1]), down)
    send("x_own_a", images.at[0:CUT, :], part(SLOT[1, 0], *a_rows), across)
    send("x_own_b", images.at[CUT:ROWS, :], part(SLOT[1, 0], *b_rows), across)
    send("s_own", images, part(SLOT[0, 0]), sibling)

    local = (partners[...] - ((ref + 8) % 16) * R).astype(F32)
    lane = lax.broadcasted_iota(jnp.int32, (128, 128), 1).astype(F32)
    for i in range(R // 128):
        column = jnp.transpose(jnp.broadcast_to(local[i:i + 1, :], (128, 128)))
        for j in range(R // 128):
            pick[i * 128:(i + 1) * 128, j * 128:(j + 1) * 128] = (column == lane + j * 128.0).astype(F32).astype(BF16)

    get_refs.wait()

    @pl.loop(0, R // 128)
    def _(i):
        block = refs[pl.ds(i * 128, 128), :].astype(F32)
        total = jnp.sum(block * block, axis=1, keepdims=True)
        norms[pl.ds(i * 128, 128), :] = jnp.broadcast_to(total * (0.5 / K), (128, UNIT))

    def scores(where, column):
        dx, dy = where
        first = ((y + dy + 4) % 4) * 4 + (h if dx == 0 else 1 - h) * 2
        table = expo if dx == 0 else expo_x
        bias = jnp.concatenate([table[pl.ds(first, 1), :], table[pl.ds(first + 1, 1), :]], axis=1)
        bias = 0.25 * bias.astype(F32)
        slot = SLOT[where]

        @pl.loop(0, 2)
        def _(i):
            r = pl.ds(pl.multiple_of(i * (R // 2), R // 2), R // 2)
            s = lax.dot_general(refs[r, :], img[slot * UNIT:(slot + 1) * UNIT, :], (((1,), (1,)), ((), ())),
                                preferred_element_type=F32)
            wts[r, column:column + UNIT] = jnp.exp(s * (1.0 / 64.0) - norms[r, :] - bias).astype(BF16)

    def column_of(dl, dz):
        return pl.ds(pl.multiple_of((((l + dl) % 2) * 4 + (z + dz) % 4) * W, W), W)

    def accumulate(slot, count, start=False):
        @pl.loop(0, 8)
        def _(j):
            added = jnp.dot(wts[:, 0:count], img[slot * UNIT:slot * UNIT + count, column_of(j // 4, j % 4)],
                            preferred_element_type=F32)
            acc[j] = added if start else acc[j] + added

    get_own.wait()
    arrived("s_own", "expo")
    scores((0, 0), 0)
    accumulate(0, UNIT, start=True)

    arrived("up_own", "down_own", "x_own_a")
    send("up_far_b", part(SLOT[0, -1], *b_rows, left), part(SLOT[0, 2], *b_rows, left), up)
    send("down_far_b", part(SLOT[0, 1], *b_rows, right), part(SLOT[0, 2], *b_rows, right), down)
    send("x_1", part(SLOT[0, 1], *b_rows), part(SLOT[1, 1], *b_rows), across)
    send("x_-1", part(SLOT[0, -1], *b_rows), part(SLOT[1, -1], *b_rows), across)
    send("up_x", part(SLOT[1, 0], *a_rows), part(SLOT[1, -1], *a_rows), up)
    send("down_x", part(SLOT[1, 0], *a_rows), part(SLOT[1, 1], *a_rows), down)
    send("up_far_a", part(SLOT[0, -1], *a_rows, left), part(SLOT[0, 2], *a_rows, left), up)
    send("down_far_a", part(SLOT[0, 1], *a_rows, right), part(SLOT[0, 2], *a_rows, right), down)
    send("s_1", part(SLOT[0, 1]), part(SLOT[0, 1]), sibling)
    send("s_2", part(SLOT[0, -1]), part(SLOT[0, -1]), sibling)
    arrived("x_own_b")
    send("s_3", part(SLOT[1, 0]), part(SLOT[1, 0]), sibling)

    arrived("s_1")
    scores((0, 1), 0)
    arrived("s_2")
    scores((0, -1), UNIT)
    arrived("s_3")
    scores((1, 0), 2 * UNIT)
    arrived("up_far_b", "down_far_b")
    send("x_2", part(SLOT[0, 2], *b_rows), part(SLOT[1, 2], *b_rows), across)
    accumulate(1, 3 * UNIT)

    arrived("up_x", "down_x")
    send("up_x_far", part(SLOT[1, -1], *a_rows, left), part(SLOT[1, 2], *a_rows, left), up)
    send("down_x_far", part(SLOT[1, 1], *a_rows, right), part(SLOT[1, 2], *a_rows, right), down)
    arrived("x_1", "x_-1")
    send("s_4", part(SLOT[1, 1]), part(SLOT[1, 1]), sibling)
    send("s_5", part(SLOT[1, -1]), part(SLOT[1, -1]), sibling)
    arrived("s_4")
    scores((1, 1), 0)
    arrived("s_5")
    scores((1, -1), UNIT)
    arrived("up_far_a", "down_far_a")
    send("s_6", part(SLOT[0, 2]), part(SLOT[0, 2]), sibling)
    accumulate(4, 2 * UNIT)
    arrived("x_2")
    send("s_7b", part(SLOT[1, 2], *b_rows), part(SLOT[1, 2], *b_rows), sibling)
    arrived("s_6")
    scores((0, 2), 0)
    arrived("up_x_far", "down_x_far")
    send("s_7a", part(SLOT[1, 2], *a_rows), part(SLOT[1, 2], *a_rows), sibling)
    accumulate(6, UNIT)
    arrived("s_7a", "s_7b")
    scores((1, 2), 0)

    A, B = slice(0, RA), slice(RA, R)
    lo, hi = slice(0, HALF), slice(HALF, W)
    for t, dz in enumerate(ORDER):
        @pl.loop(0, 2)
        def _(i):
            dl = 1 - i
            added = jnp.dot(wts[:, 0:UNIT], img[7 * UNIT:8 * UNIT, column_of(dl, dz)], preferred_element_type=F32)
            value = acc[dl * 4 + dz] + added
            acc[dl * 4 + dz] = value
            if t < 3:
                st_a[t, dl] = value[A].astype(BF16)

            @pl.when(dl == 1)
            def _():
                st_b1[t] = value[B].astype(BF16)

        send(f"b1_{t}", st_b1.at[t], r_b1.at[t], beside)
        if t == 0:
            send("a1_up", st_a.at[0, :, :, lo], r_a1.at[0], above)
            send("a1_down", st_a.at[0, :, :, hi], r_a1.at[1], below)
        if t == 1:
            send("a2_up", st_a.at[1, :, :, hi], r_a2.at[0, :, :, hi], above)
        if t == 2:
            send("a2_down", st_a.at[2, :, :, lo], r_a2.at[1, :, :, lo], below)

    arrived("a1_up")
    for dl in (1, 0):
        st_a2[0, dl] = (acc[dl * 4 + 1, A, lo] + r_a1[0, dl].astype(F32)).astype(BF16)
    send("a2d_up", st_a2.at[0], r_a2.at[0, :, :, lo], above)
    arrived("a1_down")
    for dl in (1, 0):
        st_a2[1, dl] = (acc[dl * 4 + 3, A, hi] + r_a1[1, dl].astype(F32)).astype(BF16)
    send("a2d_down", st_a2.at[1], r_a2.at[1, :, :, hi], below)

    arrived("b1_0")
    st_b2[...] = (acc[2, B, :] + r_b1[0].astype(F32)).astype(BF16)
    send("b2_up", st_b2.at[:, lo], r_b2.at[0], above)
    send("b2_down", st_b2.at[:, hi], r_b2.at[1], below)
    arrived("b1_1")
    st_b3[0] = (acc[1, B, hi] + r_b1[1, :, hi].astype(F32)).astype(BF16)
    send("b3_up", st_b3.at[0], r_b3.at[0, :, hi], above)
    arrived("b1_2")
    st_b3[1] = (acc[3, B, lo] + r_b1[2, :, lo].astype(F32)).astype(BF16)
    send("b3_down", st_b3.at[1], r_b3.at[1, :, lo], below)

    arrived("a2_up", "a2_down", "a2d_up", "a2d_down")
    st_a3[...] = (acc[4, A, :] + r_a2[0, 1].astype(F32) + r_a2[1, 1].astype(F32)).astype(BF16)
    send("a3", st_a3, r_a3, beside)

    arrived("b2_up")
    st_b3d[0] = (acc[1, B, lo] + r_b1[1, :, lo].astype(F32) + r_b2[0].astype(F32)).astype(BF16)
    send("b3d_up", st_b3d.at[0], r_b3.at[0, :, lo], above)
    arrived("b2_down")
    st_b3d[1] = (acc[3, B, hi] + r_b1[2, :, hi].astype(F32) + r_b2[1].astype(F32)).astype(BF16)
    send("b3d_down", st_b3d.at[1], r_b3.at[1, :, hi], below)

    acc[0, A, :] = acc[0, A, :] + r_a2[0, 0].astype(F32) + r_a2[1, 0].astype(F32)
    arrived("a3")
    acc[0, A, :] = acc[0, A, :] + r_a3[...].astype(F32)
    final[A, :] = acc[0, A, :].astype(BF16)
    send("p1a_up", final.at[A, lo], relay.at[0, A, :], up)
    send("p1a_down", final.at[A, hi], relay.at[1, A, :], down)
    arrived("b1_3", "b3_up", "b3_down", "b3d_up", "b3d_down")
    acc[0, B, :] = (acc[0, B, :] + r_b1[3].astype(F32)) + (r_b3[0].astype(F32) + r_b3[1].astype(F32))
    final[B, :] = acc[0, B, :].astype(BF16)
    send("p1b_up", final.at[B, lo], relay.at[0, B, :], up)
    send("p1b_down", final.at[B, hi], relay.at[1, B, :], down)
    arrived("p1a_up")
    send("p2a_up", relay.at[0, A, :], other.at[A, lo], up)
    arrived("p1a_down")
    send("p2a_down", relay.at[1, A, :], other.at[A, hi], down)
    arrived("p1b_up")
    send("p2b_up", relay.at[0, B, :], other.at[B, lo], up)
    arrived("p1b_down")
    send("p2b_down", relay.at[1, B, :], other.at[B, hi], down)
    arrived("p2a_up", "p2a_down", "p2b_up", "p2b_down")

    scale = 0.5 / 128.0

    @pl.loop(0, 2)
    def _(i):
        r = pl.ds(pl.multiple_of(i * (R // 2), R // 2), R // 2)
        theirs = jnp.dot(pick[r, :], other[...], preferred_element_type=F32)
        out[r, :] = (acc[0, r, :] + theirs) * scale

    for copy in copies.values():
        copy.wait_send()


COPIES = 80


def body(images, exponents, references, partners):
    return pl.pallas_call(
        kernel,
        out_shape=jax.ShapeDtypeStruct((R, W), F32),
        in_specs=[
            pl.BlockSpec(memory_space=pl.ANY),
            pl.BlockSpec(memory_space=pltpu.VMEM),
            pl.BlockSpec(memory_space=pl.ANY),
            pl.BlockSpec(memory_space=pltpu.VMEM),
        ],
        out_specs=pl.BlockSpec(memory_space=pltpu.VMEM),
        scratch_shapes=[
            pltpu.VMEM((8 * UNIT, K), BF16),
            pltpu.VMEM((R, K), BF16),
            pltpu.VMEM((8, R, W), F32),
            pltpu.VMEM((R, 3 * UNIT), BF16),
            pltpu.VMEM((R, UNIT), F32),
            pltpu.VMEM((R, R), BF16),
            pltpu.VMEM((16, 128), jnp.int32),
            pltpu.VMEM((3, 2, RA, W), BF16),
            pltpu.VMEM((2, 2, RA, HALF), BF16),
            pltpu.VMEM((RA, W), BF16),
            pltpu.VMEM((4, RB, W), BF16),
            pltpu.VMEM((RB, W), BF16),
            pltpu.VMEM((2, RB, HALF), BF16),
            pltpu.VMEM((2, RB, HALF), BF16),
            pltpu.VMEM((2, 2, RA, HALF), BF16),
            pltpu.VMEM((2, 2, RA, W), BF16),
            pltpu.VMEM((RA, W), BF16),
            pltpu.VMEM((4, RB, W), BF16),
            pltpu.VMEM((2, RB, HALF), BF16),
            pltpu.VMEM((2, RB, W), BF16),
            pltpu.VMEM((R, W), BF16),
            pltpu.VMEM((2, R, HALF), BF16),
            pltpu.VMEM((R, W), BF16),
            pltpu.SemaphoreType.DMA((2,)),
            pltpu.SemaphoreType.DMA((COPIES,)),
            pltpu.SemaphoreType.DMA((COPIES,)),
        ],
        compiler_params=pltpu.CompilerParams(
            collective_id=0, has_side_effects=True, vmem_limit_bytes=67043328),
    )(images, exponents.reshape(16, 128), references, partners.reshape(6, 128))


def solution(mesh):
    in_specs = (P(("img", "ref"), None), P("img"), P("ref", None), P("ref"))
    out_specs = P("ref", "img")
    return jax.shard_map(body, mesh=mesh, in_specs=in_specs, out_specs=out_specs, check_vma=False)
```

```python
import jax
import jax.numpy as jnp
from jax import lax
from jax.experimental import pallas as pl
from jax.experimental.pallas import tpu as pltpu
from jax.sharding import PartitionSpec as P

MESH = pl.DeviceIdType.MESH
F32 = jnp.float32
BF16 = jnp.bfloat16

R = 768
K = 4096
W = 512
ROWS = 128
UNIT = 256
CUT = 2304
RA = 432
RB = R - RA
HALF = W // 2
A_ROWS = (slice(0, 288), slice(288, RA))
B_ROWS = (slice(544, R), slice(RA, 544))
LATE = B_ROWS[1].stop - A_ROWS[1].start
HALVES = ROWS // 2

UNITS = (
    ((0, 0, 0), (0, 0, 1)),
    ((0, 1, 1), (0, -1, 0)),
    ((1, 0, 0), (1, 0, 1)),
    ((0, 1, 0), (0, -1, 1)),
    ((0, 2, 0), (0, 2, 1)),
    ((1, 1, 1), (1, -1, 0)),
    ((1, 1, 0), (1, -1, 1)),
    ((1, 2, 0), (1, 2, 1)),
)
BLOCK = {block: i for i, block in enumerate(block for unit in UNITS for block in unit)}
ORDER = (2, 1, 3, 0)


def kernel(images, expo_hbm, refs_hbm, partners_hbm, sums, late, pick_late, img, refs, acc, wts, norms, pick,
           expo, expo_x, table, partners, early, r_a1, r_a2, r_a3, r_b1, r_b2, r_b3,
           final, relay, other, local_sem, send_sem, recv_sem):
    ref, im = lax.axis_index("ref"), lax.axis_index("img")
    y, h, c = ref // 4, (ref // 2) % 2, ref % 2
    l, z = im // 4, im % 4

    def device(y, h, c, l, z):
        return {"ref": y * 4 + h * 2 + c, "img": l * 4 + z}

    up = device((y + 1) % 4, h, c, l, z)
    down = device((y + 3) % 4, h, c, l, z)
    across = device(y, 1 - h, c, 1 - l, z)
    sibling = device(y, h, 1 - c, l, z)
    beside = device(y, h, c, 1 - l, z)
    above = device(y, h, c, l, (z + 1) % 4)
    below = device(y, h, c, l, (z + 3) % 4)

    started = []

    def fetch(src, dst):
        started.append(pltpu.make_async_copy(src, dst, local_sem.at[len(started)]))
        started[-1].start()
        return started[-1]

    get_expo = fetch(expo_hbm, expo)
    get_partners = fetch(partners_hbm, partners)
    get_refs = fetch(refs_hbm, refs)
    get_own = [fetch(images.at[k * HALVES:(k + 1) * HALVES, :],
                     img.at[pl.ds(pl.multiple_of(k * ROWS + c * HALVES, HALVES), HALVES), :]) for k in range(2)]

    neighbours = (up, down, across, sibling, beside, above, below)
    barrier = pltpu.get_barrier_semaphore()
    for who in neighbours:
        pl.semaphore_signal(barrier, inc=1, device_id=who, device_id_type=MESH)
    pl.semaphore_wait(barrier, len(neighbours))

    copies = {}

    def send(name, src, dst, who):
        at = len(copies)
        copies[name] = pltpu.make_async_remote_copy(
            src_ref=src, dst_ref=dst, send_sem=send_sem.at[at], recv_sem=recv_sem.at[at],
            device_id=who, device_id_type=MESH)
        copies[name].start()

    def arrived(*names):
        for name in names:
            copies[name].wait_recv()

    whole, a_cols, b_cols = slice(0, K), slice(0, CUT), slice(CUT, K)

    def part(dx, dy, half, columns=whole, first=0, count=HALVES):
        return img.at[pl.ds(pl.multiple_of(BLOCK[dx, dy, half] * ROWS + c * HALVES + first, 16), count), columns]

    def own(half, columns=whole):
        return images.at[half * HALVES:(half + 1) * HALVES, columns]

    def share(dx, dy, half, columns=whole, first=0, count=HALVES):
        at = part(dx, dy, half, columns, first, count)
        name = f"s{dx}{dy}{half}_{columns.start}_{first}"
        send(name, at, at, sibling)
        return name

    for k in range(2):
        send(f"up_own{k}", own(k), part(0, -1, k), up)
        send(f"down_own{1 - k}", own(1 - k), part(0, 1, 1 - k), down)
    send("x_own_a0", own(0, a_cols), part(1, 0, 0, a_cols), across)
    send("x_own_a1", own(1, a_cols), part(1, 0, 1, a_cols), across)
    send("x_own_b0", own(0, b_cols), part(1, 0, 0, b_cols), across)
    send("x_own_b1", own(1, b_cols), part(1, 0, 1, b_cols), across)
    for k in range(2):
        send(f"s_own{k}", own(k), part(0, 0, k), sibling)
    get_expo.wait()
    send("expo", expo, expo_x, across)

    sub = lax.broadcasted_iota(jnp.int32, (16, 128), 0) % 2 == 0
    first_lanes = lax.broadcasted_iota(jnp.int32, (16, 128), 1) < HALVES

    def arrange(k, raw):
        turned = pltpu.roll(raw, HALVES, 1)
        even = jnp.where(first_lanes, raw, pltpu.roll(turned, 15, 0))
        odd = jnp.where(first_lanes, pltpu.roll(turned, 1, 0), raw)
        table[k] = jnp.where(sub, even, odd).astype(F32) * 0.25

    arrange(0, expo[...])
    get_partners.wait()
    local = (partners[...] - ((ref + 8) % 16) * R).astype(F32)
    lane = lax.broadcasted_iota(jnp.int32, (128, 128), 1) + A_ROWS[1].start
    for i in range(R // 128):
        column = jnp.transpose(jnp.broadcast_to(local[i:i + 1, :], (128, 128)))
        for j in range(R // 128):
            place = lane + j * 128
            place = jnp.where(place < R, place, place - R).astype(F32)
            pick[i * 128:(i + 1) * 128, j * 128:(j + 1) * 128] = (column == place).astype(F32).astype(BF16)

    put_pick = fetch(pick.at[:, 0:LATE], pick_late)
    get_refs.wait()

    @pl.loop(0, R // 128)
    def _(i):
        block = refs[pl.ds(i * 128, 128), :].astype(F32)
        total = jnp.sum(block * block, axis=1, keepdims=True)
        norms[pl.ds(i * 128, 128), :] = jnp.broadcast_to(total * (0.5 / K), (128, UNIT))

    def product(rows, unit, columns):
        return lax.dot_general(refs[rows, columns], img[unit * UNIT:(unit + 1) * UNIT, columns],
                               (((1,), (1,)), ((), ())), preferred_element_type=F32)

    def scores(unit, column=0, begun=False):
        bias = jnp.concatenate([
            table[dx, pl.ds((((y + dy + 4) % 4) * 2 + (h if dx == 0 else 1 - h)) * 2 + half, 1), :]
            for dx, dy, half in UNITS[unit]], axis=1)

        @pl.loop(0, 2)
        def _(i):
            r = pl.ds(pl.multiple_of(i * (R // 2), R // 2), R // 2)
            if begun:
                s = early[r, :] + product(r, unit, a_cols)
            else:
                s = product(r, unit, whole)
            wts[r, column:column + UNIT] = jnp.exp(s * (1.0 / 64.0) - norms[r, :] - bias).astype(BF16)

    def column_of(dl, dz):
        return pl.ds(pl.multiple_of((((l + dl) % 2) * 4 + (z + dz) % 4) * W, W), W)

    def accumulate(unit, units=1, start=False):
        count = units * UNIT

        @pl.loop(0, 8)
        def _(j):
            added = jnp.dot(wts[:, 0:count], img[unit * UNIT:unit * UNIT + count, column_of(j // 4, j % 4)],
                            preferred_element_type=F32)
            acc[j] = added if start else acc[j] + added

    for copy in get_own:
        copy.wait()
    arrived("s_own0", "s_own1")
    scores(0)
    accumulate(0, start=True)

    arrived("up_own0", "down_own1")
    unit_1 = [share(0, 1, 1), share(0, -1, 0)]
    send("up_far_b", part(0, -1, 0, b_cols), part(0, 2, 0, b_cols), up)
    send("down_far_b", part(0, 1, 1, b_cols), part(0, 2, 1, b_cols), down)
    send("x_-10", part(0, -1, 0, b_cols), part(1, -1, 0, b_cols), across)
    send("x_11", part(0, 1, 1, b_cols), part(1, 1, 1, b_cols), across)
    send("up_far_a", part(0, -1, 0, a_cols), part(0, 2, 0, a_cols), up)
    send("down_far_a", part(0, 1, 1, a_cols), part(0, 2, 1, a_cols), down)
    arrived(*unit_1)
    scores(1)
    accumulate(1)

    arrived("up_own1", "down_own0", "x_own_a0", "x_own_a1", "x_own_b0", "x_own_b1", "expo")
    send("x_-11", part(0, -1, 1, b_cols), part(1, -1, 1, b_cols), across)
    send("x_10", part(0, 1, 0, b_cols), part(1, 1, 0, b_cols), across)
    for k in range(2):
        send(f"up_x{k}", part(1, 0, k, a_cols), part(1, -1, k, a_cols), up)
        send(f"down_x{1 - k}", part(1, 0, 1 - k, a_cols), part(1, 1, 1 - k, a_cols), down)
    unit_2 = [share(1, 0, 0), share(1, 0, 1)]
    unit_3 = [share(0, 1, 0), share(0, -1, 1)]
    arrange(1, expo_x[...])

    arrived(*unit_2)
    scores(2)
    arrived(*unit_3)
    scores(3, UNIT)
    accumulate(2, 2)

    arrived("up_far_b", "down_far_b")
    for k in range(2):
        send(f"x_2{k}", part(0, 2, k, b_cols), part(1, 2, k, b_cols), across)
    arrived("up_far_a", "down_far_a")
    unit_4 = [share(0, 2, 0), share(0, 2, 1)]
    arrived(*unit_4)
    scores(4)
    accumulate(4)

    quarter = HALVES // 2
    arrived("up_x0", "down_x1")
    for k in range(2):
        at = (a_cols, k * quarter, quarter)
        send(f"up_x_far{k}", part(1, -1, 0, *at), part(1, 2, 0, *at), up)
        send(f"down_x_far{k}", part(1, 1, 1, *at), part(1, 2, 1, *at), down)
    arrived("x_-10", "x_11")
    unit_5 = [share(1, 1, 1), share(1, -1, 0)]
    arrived(*unit_5)
    scores(5)
    accumulate(5)
    arrived("up_x1", "down_x0", "x_-11", "x_10")
    unit_6 = [share(1, 1, 0), share(1, -1, 1)]
    arrived(*unit_6)
    scores(6)
    arrived("x_20", "x_21")
    unit_7 = [share(1, 2, k, b_cols) for k in range(2)]
    accumulate(6)
    arrived(*unit_7)

    @pl.loop(0, 2)
    def _(i):
        r = pl.ds(pl.multiple_of(i * (R // 2), R // 2), R // 2)
        early[r, :] = product(r, 7, b_cols)

    unit_7 = []
    for k in range(2):
        for half, way in enumerate(("up", "down")):
            arrived(f"{way}_x_far{k}")
            unit_7.append(share(1, 2, half, a_cols, k * quarter, quarter))
    arrived(*unit_7)
    scores(7, begun=True)

    lo, hi = slice(0, HALF), slice(HALF, W)
    AB = slice(0, RA), slice(RA, R)
    near = [slice(b.start - RA, b.stop - RA) for b in B_ROWS]

    def st_a(t, half, dl, a):
        return refs.at[a, pl.ds(pl.multiple_of(t * 1024 + half * W + dl * HALF, HALF), HALF)]

    def pair(t, half, a):
        return refs.at[a, t * 1024 + half * W:t * 1024 + half * W + W]

    def st_a2(k, a):
        return refs.at[a, 3072 + k * W:3072 + (k + 1) * W]

    def st_b(first, count, b):
        return refs.at[b, first:first + count]

    def a1(s):
        a = A_ROWS[s]
        send(f"a1_up{s}", pair(0, 0, a), r_a1.at[0, a, :], above)
        send(f"a1_down{s}", pair(0, 1, a), r_a1.at[1, a, :], below)

    def a2_up(s):
        send(f"a2_up{s}", pair(1, 1, A_ROWS[s]), r_a2.at[0, A_ROWS[s], W:2 * W], above)

    def a2_down(s):
        send(f"a2_down{s}", pair(2, 0, A_ROWS[s]), r_a2.at[1, A_ROWS[s], 0:W], below)

    def a2d(s):
        a = A_ROWS[s]
        for k, dz, cols, way, who in ((0, 1, lo, "up", above), (1, 3, hi, "down", below)):
            arrived(f"a1_{way}{s}")
            for dl in (1, 0):
                there = slice(dl * HALF, (dl + 1) * HALF)
                value = (acc[dl * 4 + dz, a, cols] + r_a1[k, a, there].astype(F32)).astype(BF16)
                refs[a, 3072 + k * W + dl * HALF:3072 + k * W + (dl + 1) * HALF] = value
            send(f"a2d_{way}{s}", st_a2(k, a), r_a2.at[k, a, k * W:(k + 1) * W], who)

    def a3(s):
        a = A_ROWS[s]
        arrived(f"a2_up{s}", f"a2_down{s}", f"a2d_up{s}", f"a2d_down{s}")
        for dl in (1, 0):
            for half, cols in enumerate((lo, hi)):
                there = slice(half * W + dl * HALF, half * W + (dl + 1) * HALF)
                value = acc[dl * 4, a, cols] + r_a2[0, a, there].astype(F32) + r_a2[1, a, there].astype(F32)
                if dl:
                    wts[a, UNIT + half * HALF:UNIT + (half + 1) * HALF] = value.astype(BF16)
                else:
                    acc[0, a, cols] = value
            if dl:
                send(f"a3_{s}", wts.at[a, UNIT:UNIT + W], r_a3.at[a, :], beside)

    def b1(s, t):
        send(f"b1_{t}{s}", st_b(t * W, W, B_ROWS[s]), r_b1.at[t, near[s], :], beside)

    def b2(s):
        b, n = B_ROWS[s], near[s]
        arrived(f"b1_0{s}")
        refs[b, 2048:2048 + W] = (acc[2, b, :] + r_b1[0, n, :].astype(F32)).astype(BF16)
        send(f"b2_up{s}", st_b(2048, HALF, b), r_b2.at[0, n, :], above)
        send(f"b2_down{s}", st_b(2048 + HALF, HALF, b), r_b2.at[1, n, :], below)

    def b3(s, k):
        b, n = B_ROWS[s], near[s]
        t, dz, cols, way, who = ((1, 1, hi, "up", above), (2, 3, lo, "down", below))[k]
        arrived(f"b1_{t}{s}")
        first = 2560 + k * HALF
        refs[b, first:first + HALF] = (acc[dz, b, cols] + r_b1[t, n, cols].astype(F32)).astype(BF16)
        send(f"b3_{way}{s}", st_b(first, HALF, b), r_b3.at[k, n, cols], who)

    def b3d(s):
        b, n = B_ROWS[s], near[s]
        for k, t, dz, cols, way, who in ((0, 1, 1, lo, "up", above), (1, 2, 3, hi, "down", below)):
            arrived(f"b2_{way}{s}")
            value = acc[dz, b, cols] + r_b1[t, n, cols].astype(F32) + r_b2[k, n, :].astype(F32)
            first = 3072 + k * HALF
            refs[b, first:first + HALF] = value.astype(BF16)
            send(f"b3d_{way}{s}", st_b(first, HALF, b), r_b3.at[k, n, cols], who)

    def finish(name, rows):
        final[rows, :] = acc[0, rows, :].astype(BF16)
        send(f"p1_up_{name}", final.at[rows, lo], relay.at[0, rows, :], up)
        send(f"p1_down_{name}", final.at[rows, hi], relay.at[1, rows, :], down)

    def finish_a(s):
        a = A_ROWS[s]
        arrived(f"a3_{s}")
        acc[0, a, :] = acc[0, a, :] + r_a3[a, :].astype(F32)
        finish(f"a{s}", a)

    def finish_b(s):
        b, n = B_ROWS[s], near[s]
        arrived(f"b1_3{s}", f"b3_up{s}", f"b3_down{s}", f"b3d_up{s}", f"b3d_down{s}")
        acc[0, b, :] = (acc[0, b, :] + r_b1[3, n, :].astype(F32)) + (r_b3[0, n, :].astype(F32) + r_b3[1, n, :].astype(F32))
        finish(f"b{s}", b)

    def pass_on(name, rows, stage):
        first = (rows.start - A_ROWS[1].start) % R
        there = slice(first, first + rows.stop - rows.start) if stage else slice(first - LATE, first - LATE + rows.stop - rows.start)
        dst = late if stage else other
        arrived(f"p1_up_{name}")
        send(f"p2_up_{name}", relay.at[0, rows, :], dst.at[there, lo], up)
        arrived(f"p1_down_{name}")
        send(f"p2_down_{name}", relay.at[1, rows, :], dst.at[there, hi], down)

    for t, dz in enumerate(ORDER):
        @pl.loop(0, 2)
        def _(i):
            dl = 1 - i
            added = jnp.dot(wts[:, 0:UNIT], img[7 * UNIT:8 * UNIT, column_of(dl, dz)], preferred_element_type=F32)
            value = acc[dl * 4 + dz] + added
            acc[dl * 4 + dz] = value
            if t < 3:
                for half, cols in enumerate((lo, hi)):
                    st_a(t, half, dl, AB[0])[...] = value[AB[0], cols].astype(BF16)

            @pl.when(dl == 1)
            def _():
                refs[AB[1], t * W:(t + 1) * W] = value[AB[1]].astype(BF16)

        b1(0, t)
        if t == 0:
            a1(0)
        if t == 1:
            a2_up(0)
        if t == 2:
            a2_down(0)

    a2d(0)
    b2(0)
    b3(0, 0)
    b3(0, 1)
    a3(0)
    for t in range(4):
        b1(1, t)
    b3d(0)
    a1(1)
    a2_up(1)
    a2_down(1)
    finish_a(0)
    finish_b(0)
    a2d(1)
    b2(1)
    b3(1, 0)
    pass_on("a0", A_ROWS[0], 0)
    pass_on("b0", B_ROWS[0], 0)
    b3(1, 1)
    a3(1)
    b3d(1)
    finish_b(1)
    finish_a(1)
    pass_on("b1", B_ROWS[1], 1)
    pass_on("a1", A_ROWS[1], 1)

    arrived("p2_up_a0", "p2_down_a0", "p2_up_b0", "p2_down_b0")
    puts = []
    for i in range(2):
        r = slice(i * (R // 2), (i + 1) * (R // 2))
        acc[0, r, :] = acc[0, r, :] + jnp.dot(pick[r, LATE:R], other[...], preferred_element_type=F32)
        puts.append(fetch(acc.at[0, r, :], sums.at[r, :]))
    arrived("p2_up_b1", "p2_down_b1", "p2_up_a1", "p2_down_a1")
    for copy in copies.values():
        copy.wait_send()
    for copy in [put_pick] + puts:
        copy.wait()


PARTS = 4


def average(pick_hbm, late_hbm, sums_hbm, out_hbm, pick, late, sums, out, in_sem, out_sem):
    rows = [slice(i * (R // PARTS), (i + 1) * (R // PARTS)) for i in range(PARTS)]
    fetches = [pltpu.make_async_copy(late_hbm, late, in_sem.at[PARTS]),
               pltpu.make_async_copy(pick_hbm, pick, in_sem.at[PARTS + 1])]
    fetches += [pltpu.make_async_copy(sums_hbm.at[r, :], sums.at[r, :], in_sem.at[i]) for i, r in enumerate(rows)]
    for copy in fetches:
        copy.start()
    fetches[0].wait()
    fetches[1].wait()
    puts = []
    for i, r in enumerate(rows):
        theirs = jnp.dot(pick[r, :], late[...], preferred_element_type=F32)
        fetches[2 + i].wait()
        out[r, :] = (sums[r, :] + theirs) * (0.5 / 128.0)
        puts.append(pltpu.make_async_copy(out.at[r, :], out_hbm.at[r, :], out_sem.at[i]))
        puts[-1].start()
    for copy in puts:
        copy.wait()


COPIES = 112
VMEM = 67043328


def body(images, exponents, references, partners):
    anywhere = pl.BlockSpec(memory_space=pl.ANY)
    sums, late, pick = pl.pallas_call(
        kernel,
        out_shape=(jax.ShapeDtypeStruct((R, W), F32), jax.ShapeDtypeStruct((LATE, W), BF16),
                   jax.ShapeDtypeStruct((R, LATE), BF16)),
        in_specs=[anywhere] * 4,
        out_specs=(anywhere,) * 3,
        scratch_shapes=[
            pltpu.VMEM((8 * UNIT, K), BF16),
            pltpu.VMEM((R, K), BF16),
            pltpu.VMEM((8, R, W), F32),
            pltpu.VMEM((R, 3 * UNIT), BF16),
            pltpu.VMEM((R, UNIT), F32),
            pltpu.VMEM((R, R), BF16),
            pltpu.VMEM((16, 128), jnp.int32),
            pltpu.VMEM((16, 128), jnp.int32),
            pltpu.VMEM((2, 16, 128), F32),
            pltpu.VMEM((6, 128), jnp.int32),
            pltpu.VMEM((R, UNIT), F32),
            pltpu.VMEM((2, RA, W), BF16),
            pltpu.VMEM((2, RA, 2 * W), BF16),
            pltpu.VMEM((RA, W), BF16),
            pltpu.VMEM((4, RB, W), BF16),
            pltpu.VMEM((2, RB, HALF), BF16),
            pltpu.VMEM((2, RB, W), BF16),
            pltpu.VMEM((R, W), BF16),
            pltpu.VMEM((2, R, HALF), BF16),
            pltpu.VMEM((R - LATE, W), BF16),
            pltpu.SemaphoreType.DMA((16,)),
            pltpu.SemaphoreType.DMA((COPIES,)),
            pltpu.SemaphoreType.DMA((COPIES,)),
        ],
        compiler_params=pltpu.CompilerParams(
            collective_id=0, has_side_effects=True, vmem_limit_bytes=VMEM),
    )(images, exponents.reshape(16, 128), references, partners.reshape(6, 128))
    return pl.pallas_call(
        average,
        out_shape=jax.ShapeDtypeStruct((R, W), F32),
        in_specs=[anywhere] * 3,
        out_specs=anywhere,
        scratch_shapes=[
            pltpu.VMEM((R, LATE), BF16),
            pltpu.VMEM((LATE, W), BF16),
            pltpu.VMEM((R, W), F32),
            pltpu.VMEM((R, W), F32),
            pltpu.SemaphoreType.DMA((PARTS + 2,)),
            pltpu.SemaphoreType.DMA((PARTS,)),
        ],
        compiler_params=pltpu.CompilerParams(vmem_limit_bytes=67043328),
    )(pick, late, sums)


def solution(mesh):
    in_specs = (P(("img", "ref"), None), P("img"), P("ref", None), P("ref"))
    out_specs = P("ref", "img")
    return jax.shard_map(body, mesh=mesh, in_specs=in_specs, out_specs=out_specs, check_vma=False)
```

```python
import math

import jax
import jax.numpy as jnp
from jax import lax
from jax.experimental import pallas as pl
from jax.experimental.pallas import tpu as pltpu
from jax.sharding import PartitionSpec as P

MESH = pl.DeviceIdType.MESH
F32 = jnp.float32
BF16 = jnp.bfloat16

R = 768
K = 4096
W = 512
ROWS = 128
UNIT = 256
CUT = 2304
RA = 416
RB = R - RA
HALF = W // 2
A_ROWS = (slice(0, 240), slice(240, 352), slice(352, 416))
B_ROWS = (slice(528, 768), slice(480, 528), slice(416, 480))
LAST = len(A_ROWS) - 1
LATE = B_ROWS[LAST].stop - A_ROWS[LAST].start
HALVES = ROWS // 2
FLIGHT = 32
GROUPS = 56

UNITS = (
    ((0, 0, 0), (0, 0, 1)),
    ((0, 1, 1), (0, -1, 0)),
    ((1, 0, 0), (1, 0, 1)),
    ((0, 1, 0), (0, -1, 1)),
    ((0, 2, 0), (0, 2, 1)),
    ((1, 1, 1), (1, -1, 0)),
    ((1, 1, 0), (1, -1, 1)),
    ((1, 2, 0), (1, 2, 1)),
)
BLOCK = {block: i for i, block in enumerate(block for unit in UNITS for block in unit)}
ORDER = (2, 1, 3, 0)


def kernel(images, expo_hbm, refs_hbm, partners_hbm, sums, late, pick_late, img, refs, acc, wts, norms, pick,
           expo, expo_x, table, partners, early, r_a1, r_a2, r_a3, r_b1, r_b2, r_b3,
           final, relay, other, local_sem, send_sem, recv_sem, expo_sem):
    ref, im = lax.axis_index("ref"), lax.axis_index("img")
    y, h, c = ref // 4, (ref // 2) % 2, ref % 2
    l, z = im // 4, im % 4

    def device(y, h, c, l, z):
        return {"ref": y * 4 + h * 2 + c, "img": l * 4 + z}

    up = device((y + 1) % 4, h, c, l, z)
    down = device((y + 3) % 4, h, c, l, z)
    across = device(y, 1 - h, c, 1 - l, z)
    sibling = device(y, h, 1 - c, l, z)
    beside = device(y, h, c, 1 - l, z)
    above = device(y, h, c, l, (z + 1) % 4)
    below = device(y, h, c, l, (z + 3) % 4)

    started = []

    def fetch(src, dst):
        started.append(pltpu.make_async_copy(src, dst, local_sem.at[len(started)]))
        started[-1].start()
        return started[-1]

    get_expo = fetch(expo_hbm, expo)
    get_partners = fetch(partners_hbm, partners)
    get_refs = fetch(refs_hbm, refs)
    get_own = [fetch(images.at[k * HALVES:(k + 1) * HALVES, :],
                     img.at[pl.ds(pl.multiple_of(k * ROWS + c * HALVES, HALVES), HALVES), :]) for k in range(2)]

    neighbours = (up, down, across, sibling, beside, above, below)
    barrier = pltpu.get_barrier_semaphore()
    for who in neighbours:
        pl.semaphore_signal(barrier, inc=1, device_id=who, device_id_type=MESH)
    pl.semaphore_wait(barrier, len(neighbours))

    copies, groups = [], {}

    def send(group, src, dst, who):
        at = len(copies)
        if at >= FLIGHT:
            copies[at - FLIGHT].wait_send()
        place, sizes = groups.setdefault(group, (len(groups), []))
        copies.append(pltpu.make_async_remote_copy(
            src_ref=src, dst_ref=dst, send_sem=send_sem.at[at % FLIGHT], recv_sem=recv_sem.at[place],
            device_id=who, device_id_type=MESH))
        copies[-1].start()
        sizes.append(math.prod(dst.shape))

    def arrived(*names):
        for name in names:
            place, sizes = groups[name]
            tiles = sum(sizes) // (16 * 128)
            wide = max(k for k in range(1, K // 128 + 1) if tiles % k == 0)
            view = img.at[0:tiles // wide * 16, 0:wide * 128]
            pltpu.make_async_remote_copy(
                src_ref=view, dst_ref=view, send_sem=send_sem.at[0], recv_sem=recv_sem.at[place],
                device_id=sibling, device_id_type=MESH).wait_recv()

    whole, a_cols, b_cols = slice(0, K), slice(0, CUT), slice(CUT, K)

    def part(dx, dy, half, columns=whole, first=0, count=HALVES):
        return img.at[pl.ds(pl.multiple_of(BLOCK[dx, dy, half] * ROWS + c * HALVES + first, 16), count), columns]

    def own(half, columns=whole):
        return images.at[half * HALVES:(half + 1) * HALVES, columns]

    def share(group, blocks, *where):
        for block in blocks:
            at = part(*block, *where)
            send(group, at, at, sibling)

    for k in range(2):
        send(f"own_{k}", own(k), part(0, -1, k), up)
        send(f"own_{k}", own(1 - k), part(0, 1, 1 - k), down)
    for cols in (a_cols, b_cols):
        for k in range(2):
            send("own_1", own(k, cols), part(1, 0, k, cols), across)
    for k in range(2):
        send("s0", own(k), part(0, 0, k), sibling)
    get_expo.wait()
    give_expo = pltpu.make_async_remote_copy(
        src_ref=expo, dst_ref=expo_x, send_sem=expo_sem.at[0], recv_sem=expo_sem.at[1],
        device_id=across, device_id_type=MESH)
    give_expo.start()

    sub = lax.broadcasted_iota(jnp.int32, (16, 128), 0) % 2 == 0
    first_lanes = lax.broadcasted_iota(jnp.int32, (16, 128), 1) < HALVES

    def arrange(k, raw):
        turned = pltpu.roll(raw, HALVES, 1)
        even = jnp.where(first_lanes, raw, pltpu.roll(turned, 15, 0))
        odd = jnp.where(first_lanes, pltpu.roll(turned, 1, 0), raw)
        table[k] = jnp.where(sub, even, odd).astype(F32) * 0.25

    arrange(0, expo[...])
    get_partners.wait()
    local = (partners[...] - ((ref + 8) % 16) * R).astype(F32)
    lane = lax.broadcasted_iota(jnp.int32, (128, 128), 1) + A_ROWS[LAST].start
    for i in range(R // 128):
        column = jnp.transpose(jnp.broadcast_to(local[i:i + 1, :], (128, 128)))
        for j in range(R // 128):
            place = lane + j * 128
            place = jnp.where(place < R, place, place - R).astype(F32)
            pick[i * 128:(i + 1) * 128, j * 128:(j + 1) * 128] = (column == place).astype(F32).astype(BF16)

    put_pick = fetch(pick.at[:, 0:LATE], pick_late)
    get_refs.wait()

    @pl.loop(0, R // 128)
    def _(i):
        block = refs[pl.ds(i * 128, 128), :].astype(F32)
        total = jnp.sum(block * block, axis=1, keepdims=True)
        norms[pl.ds(i * 128, 128), :] = jnp.broadcast_to(total * (0.5 / K), (128, UNIT))

    def product(rows, unit, columns):
        return lax.dot_general(refs[rows, columns], img[unit * UNIT:(unit + 1) * UNIT, columns],
                               (((1,), (1,)), ((), ())), preferred_element_type=F32)

    def scores(unit, column=0, begun=False):
        bias = jnp.concatenate([
            table[dx, pl.ds((((y + dy + 4) % 4) * 2 + (h if dx == 0 else 1 - h)) * 2 + half, 1), :]
            for dx, dy, half in UNITS[unit]], axis=1)

        @pl.loop(0, 2)
        def _(i):
            r = pl.ds(pl.multiple_of(i * (R // 2), R // 2), R // 2)
            if begun:
                s = early[r, :] + product(r, unit, a_cols)
            else:
                s = product(r, unit, whole)
            wts[r, column:column + UNIT] = jnp.exp(s * (1.0 / 64.0) - norms[r, :] - bias).astype(BF16)

    def column_of(dl, dz):
        return pl.ds(pl.multiple_of((((l + dl) % 2) * 4 + (z + dz) % 4) * W, W), W)

    def accumulate(unit, units=1, start=False, half=None):
        count = units * UNIT
        bounds = (0, 8) if half is None else (half * 4, half * 4 + 4)

        @pl.loop(*bounds)
        def _(j):
            added = jnp.dot(wts[:, 0:count], img[unit * UNIT:unit * UNIT + count, column_of(j // 4, j % 4)],
                            preferred_element_type=F32)
            acc[j] = added if start else acc[j] + added

    for copy in get_own:
        copy.wait()
    arrived("s0")
    scores(0)
    accumulate(0, start=True)

    arrived("own_0")
    share("s1", UNITS[1])
    send("far_b", part(0, -1, 0, b_cols), part(0, 2, 0, b_cols), up)
    send("far_b", part(0, 1, 1, b_cols), part(0, 2, 1, b_cols), down)
    send("x_5", part(0, -1, 0, b_cols), part(1, -1, 0, b_cols), across)
    send("x_5", part(0, 1, 1, b_cols), part(1, 1, 1, b_cols), across)
    send("far_a", part(0, -1, 0, a_cols), part(0, 2, 0, a_cols), up)
    send("far_a", part(0, 1, 1, a_cols), part(0, 2, 1, a_cols), down)
    arrived("s1")
    scores(1)
    accumulate(1)

    arrived("own_1")
    send("x_6", part(0, -1, 1, b_cols), part(1, -1, 1, b_cols), across)
    send("x_6", part(0, 1, 0, b_cols), part(1, 1, 0, b_cols), across)
    for k in range(2):
        send(f"y_{5 + k}", part(1, 0, k, a_cols), part(1, -1, k, a_cols), up)
        send(f"y_{5 + k}", part(1, 0, 1 - k, a_cols), part(1, 1, 1 - k, a_cols), down)
    share("s2", UNITS[2])
    share("s3", UNITS[3])
    give_expo.wait()
    arrange(1, expo_x[...])

    arrived("s2")
    scores(2)
    arrived("s3")
    scores(3, UNIT)
    accumulate(2, 2, half=0)
    arrived("far_b")
    for k in range(2):
        send("x_7", part(0, 2, k, b_cols), part(1, 2, k, b_cols), across)
    share("s4", UNITS[4], b_cols)
    arrived("x_5")
    share("s5", UNITS[5], b_cols)
    accumulate(2, 2, half=1)

    arrived("far_a")
    share("s4", UNITS[4], a_cols)
    arrived("s4")
    scores(4)
    accumulate(4, half=0)
    arrived("y_5")
    quarter = HALVES // 2
    for k in range(2):
        at = (a_cols, k * quarter, quarter)
        send(f"y_7{k}", part(1, -1, 0, *at), part(1, 2, 0, *at), up)
        send(f"y_7{k}", part(1, 1, 1, *at), part(1, 2, 1, *at), down)
    share("s5", UNITS[5], a_cols)
    accumulate(4, half=1)
    arrived("s5")
    scores(5)
    arrived("x_6")
    share("s6", UNITS[6], b_cols)
    accumulate(5, half=0)
    arrived("y_6")
    share("s6", UNITS[6], a_cols)
    accumulate(5, half=1)
    arrived("s6")
    scores(6)
    accumulate(6, half=0)
    arrived("x_7")
    share("s7b", UNITS[7], b_cols)
    arrived("y_70")
    share("s7a", UNITS[7], a_cols, 0, quarter)
    arrived("y_71")
    share("s7a", UNITS[7], a_cols, quarter, quarter)
    accumulate(6, half=1)
    arrived("s7b")

    @pl.loop(0, 2)
    def _(i):
        r = pl.ds(pl.multiple_of(i * (R // 2), R // 2), R // 2)
        early[r, :] = product(r, 7, b_cols)

    arrived("s7a")
    scores(7, begun=True)

    lo, hi = slice(0, HALF), slice(HALF, W)
    AB = slice(0, RA), slice(RA, R)
    near = [slice(b.start - RA, b.stop - RA) for b in B_ROWS]

    def st_a(t, half, dl, a):
        return refs.at[a, pl.ds(pl.multiple_of(t * 1024 + half * W + dl * HALF, HALF), HALF)]

    def pair(t, half, a):
        return refs.at[a, t * 1024 + half * W:t * 1024 + half * W + W]

    def st_a2(k, a):
        return refs.at[a, 3072 + k * W:3072 + (k + 1) * W]

    def st_b(first, count, b):
        return refs.at[b, first:first + count]

    def a1(s):
        a = A_ROWS[s]
        send(f"a1{s}", pair(0, 0, a), r_a1.at[0, a, :], above)
        send(f"a1{s}", pair(0, 1, a), r_a1.at[1, a, :], below)

    def a2(s, up=True, down=True):
        if up:
            send(f"a2{s}", pair(1, 1, A_ROWS[s]), r_a2.at[0, A_ROWS[s], W:2 * W], above)
        if down:
            send(f"a2{s}", pair(2, 0, A_ROWS[s]), r_a2.at[1, A_ROWS[s], 0:W], below)

    def a2d(s):
        a = A_ROWS[s]
        arrived(f"a1{s}")
        for k, dz, cols, who in ((0, 1, lo, above), (1, 3, hi, below)):
            for dl in (1, 0):
                there = slice(dl * HALF, (dl + 1) * HALF)
                value = (acc[dl * 4 + dz, a, cols] + r_a1[k, a, there].astype(F32)).astype(BF16)
                refs[a, 3072 + k * W + dl * HALF:3072 + k * W + (dl + 1) * HALF] = value
            send(f"a2{s}", st_a2(k, a), r_a2.at[k, a, k * W:(k + 1) * W], who)

    def a3(s):
        a = A_ROWS[s]
        arrived(f"a2{s}")
        for dl in (1, 0):
            for half, cols in enumerate((lo, hi)):
                there = slice(half * W + dl * HALF, half * W + (dl + 1) * HALF)
                value = acc[dl * 4, a, cols] + r_a2[0, a, there].astype(F32) + r_a2[1, a, there].astype(F32)
                if dl:
                    wts[a, UNIT + half * HALF:UNIT + (half + 1) * HALF] = value.astype(BF16)
                else:
                    acc[0, a, cols] = value
            if dl:
                send(f"a3_{s}", wts.at[a, UNIT:UNIT + W], r_a3.at[a, :], beside)

    def b1(s, t):
        send(f"b1_{t}{s}" if t < 3 else f"b3{s}", st_b(t * W, W, B_ROWS[s]), r_b1.at[t, near[s], :], beside)

    def b2(s):
        b, n = B_ROWS[s], near[s]
        arrived(f"b1_0{s}")
        refs[b, 2048:2048 + W] = (acc[2, b, :] + r_b1[0, n, :].astype(F32)).astype(BF16)
        send(f"b2{s}", st_b(2048, HALF, b), r_b2.at[0, n, :], above)
        send(f"b2{s}", st_b(2048 + HALF, HALF, b), r_b2.at[1, n, :], below)

    def b3(s, k):
        b, n = B_ROWS[s], near[s]
        t, dz, cols, who = ((1, 1, hi, above), (2, 3, lo, below))[k]
        arrived(f"b1_{t}{s}")
        first = 2560 + k * HALF
        refs[b, first:first + HALF] = (acc[dz, b, cols] + r_b1[t, n, cols].astype(F32)).astype(BF16)
        send(f"b3{s}", st_b(first, HALF, b), r_b3.at[k, n, cols], who)

    def b3d(s):
        b, n = B_ROWS[s], near[s]
        arrived(f"b2{s}")
        for k, t, dz, cols, who in ((0, 1, 1, lo, above), (1, 2, 3, hi, below)):
            value = acc[dz, b, cols] + r_b1[t, n, cols].astype(F32) + r_b2[k, n, :].astype(F32)
            first = 3072 + k * HALF
            refs[b, first:first + HALF] = value.astype(BF16)
            send(f"b3{s}", st_b(first, HALF, b), r_b3.at[k, n, cols], who)

    def finish(name, rows):
        final[rows, :] = acc[0, rows, :].astype(BF16)
        send(f"p1_{name}", final.at[rows, lo], relay.at[0, rows, :], up)
        send(f"p1_{name}", final.at[rows, hi], relay.at[1, rows, :], down)

    def finish_a(s):
        a = A_ROWS[s]
        arrived(f"a3_{s}")
        acc[0, a, :] = acc[0, a, :] + r_a3[a, :].astype(F32)
        finish(f"a{s}", a)

    def finish_b(s):
        b, n = B_ROWS[s], near[s]
        arrived(f"b3{s}")
        acc[0, b, :] = (acc[0, b, :] + r_b1[3, n, :].astype(F32)) + (r_b3[0, n, :].astype(F32) + r_b3[1, n, :].astype(F32))
        finish(f"b{s}", b)

    def pass_on(name, rows, s):
        first = (rows.start - A_ROWS[LAST].start) % R - (0 if s == LAST else LATE)
        there = slice(first, first + rows.stop - rows.start)
        dst = late if s == LAST else other
        arrived(f"p1_{name}")
        send(f"p2_{s == LAST}", relay.at[0, rows, :], dst.at[there, lo], up)
        send(f"p2_{s == LAST}", relay.at[1, rows, :], dst.at[there, hi], down)

    for t, dz in enumerate(ORDER):
        @pl.loop(0, 2)
        def _(i):
            dl = 1 - i
            added = jnp.dot(wts[:, 0:UNIT], img[7 * UNIT:8 * UNIT, column_of(dl, dz)], preferred_element_type=F32)
            value = acc[dl * 4 + dz] + added
            acc[dl * 4 + dz] = value
            if t < 3:
                for half, cols in enumerate((lo, hi)):
                    st_a(t, half, dl, AB[0])[...] = value[AB[0], cols].astype(BF16)

            @pl.when(dl == 1)
            def _():
                refs[AB[1], t * W:(t + 1) * W] = value[AB[1]].astype(BF16)

        b1(0, t)
        if t == 0:
            a1(0)
        if t == 1:
            a2(0, down=False)
        if t == 2:
            a2(0, up=False)

    a2d(0)
    b2(0)
    b3(0, 0)
    a3(0)
    b3(0, 1)
    a1(1)
    b3d(0)
    a2(1)
    b1(1, 0)
    b1(1, 1)
    a2d(1)
    b1(1, 2)
    b1(1, 3)
    b1(2, 0)
    finish_b(0)
    a1(2)
    finish_a(0)
    b1(2, 1)
    b2(1)
    a2(2)
    b3(1, 0)
    b1(2, 2)
    b3(1, 1)
    b1(2, 3)
    a3(1)
    pass_on("b0", B_ROWS[0], 0)
    b2(2)
    a2d(2)
    b3d(1)
    b3(2, 0)
    pass_on("a0", A_ROWS[0], 0)
    b3(2, 1)
    b3d(2)
    a3(2)
    finish_b(1)
    finish_a(1)
    finish_b(2)
    pass_on("b1", B_ROWS[1], 1)
    finish_a(2)
    pass_on("a1", A_ROWS[1], 1)
    pass_on("b2", B_ROWS[2], 2)
    pass_on("a2", A_ROWS[2], 2)

    arrived("p2_False")
    puts = []
    for i in range(2):
        r = slice(i * (R // 2), (i + 1) * (R // 2))
        acc[0, r, :] = acc[0, r, :] + jnp.dot(pick[r, LATE:R], other[...], preferred_element_type=F32)
        puts.append(fetch(acc.at[0, r, :], sums.at[r, :]))
    arrived("p2_True")
    for copy in copies[-FLIGHT:]:
        copy.wait_send()
    for copy in [put_pick] + puts:
        copy.wait()


PARTS = 4


def average(pick_hbm, late_hbm, sums_hbm, out_hbm, pick, late, sums, out, in_sem, out_sem):
    rows = [slice(i * (R // PARTS), (i + 1) * (R // PARTS)) for i in range(PARTS)]
    fetches = [pltpu.make_async_copy(late_hbm, late, in_sem.at[PARTS]),
               pltpu.make_async_copy(pick_hbm, pick, in_sem.at[PARTS + 1])]
    fetches += [pltpu.make_async_copy(sums_hbm.at[r, :], sums.at[r, :], in_sem.at[i]) for i, r in enumerate(rows)]
    for copy in fetches:
        copy.start()
    fetches[0].wait()
    fetches[1].wait()
    puts = []
    for i, r in enumerate(rows):
        theirs = jnp.dot(pick[r, :], late[...], preferred_element_type=F32)
        fetches[2 + i].wait()
        out[r, :] = (sums[r, :] + theirs) * (0.5 / 128.0)
        puts.append(pltpu.make_async_copy(out.at[r, :], out_hbm.at[r, :], out_sem.at[i]))
        puts[-1].start()
    for copy in puts:
        copy.wait()


VMEM = 67043328


def body(images, exponents, references, partners):
    anywhere = pl.BlockSpec(memory_space=pl.ANY)
    sums, late, pick = pl.pallas_call(
        kernel,
        out_shape=(jax.ShapeDtypeStruct((R, W), F32), jax.ShapeDtypeStruct((LATE, W), BF16),
                   jax.ShapeDtypeStruct((R, LATE), BF16)),
        in_specs=[anywhere] * 4,
        out_specs=(anywhere,) * 3,
        scratch_shapes=[
            pltpu.VMEM((8 * UNIT, K), BF16),
            pltpu.VMEM((R, K), BF16),
            pltpu.VMEM((8, R, W), F32),
            pltpu.VMEM((R, 3 * UNIT), BF16),
            pltpu.VMEM((R, UNIT), F32),
            pltpu.VMEM((R, R), BF16),
            pltpu.VMEM((16, 128), jnp.int32),
            pltpu.VMEM((16, 128), jnp.int32),
            pltpu.VMEM((2, 16, 128), F32),
            pltpu.VMEM((6, 128), jnp.int32),
            pltpu.VMEM((R, UNIT), F32),
            pltpu.VMEM((2, RA, W), BF16),
            pltpu.VMEM((2, RA, 2 * W), BF16),
            pltpu.VMEM((RA, W), BF16),
            pltpu.VMEM((4, RB, W), BF16),
            pltpu.VMEM((2, RB, HALF), BF16),
            pltpu.VMEM((2, RB, W), BF16),
            pltpu.VMEM((R, W), BF16),
            pltpu.VMEM((2, R, HALF), BF16),
            pltpu.VMEM((R - LATE, W), BF16),
            pltpu.SemaphoreType.DMA((8,)),
            pltpu.SemaphoreType.DMA((FLIGHT,)),
            pltpu.SemaphoreType.DMA((GROUPS,)),
            pltpu.SemaphoreType.DMA((2,)),
        ],
        compiler_params=pltpu.CompilerParams(
            collective_id=0, has_side_effects=True, vmem_limit_bytes=VMEM),
    )(images, exponents.reshape(16, 128), references, partners.reshape(6, 128))
    return pl.pallas_call(
        average,
        out_shape=jax.ShapeDtypeStruct((R, W), F32),
        in_specs=[anywhere] * 3,
        out_specs=anywhere,
        scratch_shapes=[
            pltpu.VMEM((R, LATE), BF16),
            pltpu.VMEM((LATE, W), BF16),
            pltpu.VMEM((R, W), F32),
            pltpu.VMEM((R, W), F32),
            pltpu.SemaphoreType.DMA((PARTS + 2,)),
            pltpu.SemaphoreType.DMA((PARTS,)),
        ],
        compiler_params=pltpu.CompilerParams(vmem_limit_bytes=67043328),
    )(pick, late, sums)


def solution(mesh):
    in_specs = (P(("img", "ref"), None), P("img"), P("ref", None), P("ref"))
    out_specs = P("ref", "img")
    return jax.shard_map(body, mesh=mesh, in_specs=in_specs, out_specs=out_specs, check_vma=False)
```

```python
import math

import jax
import jax.numpy as jnp
from jax import lax
from jax.experimental import pallas as pl
from jax.experimental.pallas import tpu as pltpu
from jax.sharding import PartitionSpec as P

MESH = pl.DeviceIdType.MESH
F32 = jnp.float32
BF16 = jnp.bfloat16

R = 768
K = 4096
W = 512
ROWS = 128
UNIT = 256
CUT = 2304
RA = 416
RB = R - RA
HALF = W // 2
A_ROWS = (slice(0, 240), slice(240, 352), slice(352, 416))
B_ROWS = (slice(624, 768), slice(480, 624), slice(416, 480))
LAST = len(A_ROWS) - 1
EARLY_ROWS = slice(A_ROWS[LAST].start, B_ROWS[LAST].stop)
LATE = EARLY_ROWS.stop - EARLY_ROWS.start
ORDERED = [rows for s in (2, 1, 0) for rows in (A_ROWS[s], B_ROWS[s])]
PLACE = {}
for rows in ORDERED:
    PLACE[rows.start] = sum(rows.stop - rows.start for rows in ORDERED[:len(PLACE)])
HALVES = ROWS // 2
FLIGHT = 32
GROUPS = 60

UNITS = (
    ((0, 0, 0), (0, 0, 1)),
    ((0, 1, 1), (0, -1, 0)),
    ((1, 0, 0), (1, 0, 1)),
    ((0, 1, 0), (0, -1, 1)),
    ((0, 2, 0), (0, 2, 1)),
    ((1, 1, 1), (1, -1, 0)),
    ((1, 1, 0), (1, -1, 1)),
    ((1, 2, 0), (1, 2, 1)),
)
BLOCK = {block: i for i, block in enumerate(block for unit in UNITS for block in unit)}
ORDER = (2, 1, 3, 0)


def kernel(images, expo_hbm, refs_hbm, partners_hbm, sums, late, pick_late, img, raw, refs, acc, wts, norms, pick, turn,
           expo, expo_x, table, partners, early, r_a1, r_a2, r_a3, r_b1, r_b2, r_b3,
           c_out, c_pass, c_in, final, relay, other, high, rest, local_sem, send_sem, recv_sem, expo_sem):
    ref, im = lax.axis_index("ref"), lax.axis_index("img")
    y, h, c = ref // 4, (ref // 2) % 2, ref % 2
    l, z = im // 4, im % 4

    def device(y, h, c, l, z):
        return {"ref": y * 4 + h * 2 + c, "img": l * 4 + z}

    up = device((y + 1) % 4, h, c, l, z)
    down = device((y + 3) % 4, h, c, l, z)
    across = device(y, 1 - h, c, 1 - l, z)
    sibling = device(y, h, 1 - c, l, z)
    beside = device(y, h, c, 1 - l, z)
    above = device(y, h, c, l, (z + 1) % 4)
    below = device(y, h, c, l, (z + 3) % 4)

    started = []

    def fetch(src, dst):
        started.append(pltpu.make_async_copy(src, dst, local_sem.at[len(started)]))
        started[-1].start()
        return started[-1]

    get_expo = fetch(expo_hbm, expo)
    get_partners = fetch(partners_hbm, partners)
    get_refs = fetch(refs_hbm, raw)
    get_own = [fetch(images.at[k * HALVES:(k + 1) * HALVES, :],
                     img.at[pl.ds(pl.multiple_of(k * ROWS + c * HALVES, HALVES), HALVES), :]) for k in range(2)]

    neighbours = (up, down, across, sibling, beside, above, below)
    barrier = pltpu.get_barrier_semaphore()
    for who in neighbours:
        pl.semaphore_signal(barrier, inc=1, device_id=who, device_id_type=MESH)
    pl.semaphore_wait(barrier, len(neighbours))

    copies, groups = [], {}

    def send(group, src, dst, who):
        at = len(copies)
        if at >= FLIGHT:
            copies[at - FLIGHT].wait_send()
        place, sizes = groups.setdefault(group, (len(groups), []))
        copies.append(pltpu.make_async_remote_copy(
            src_ref=src, dst_ref=dst, send_sem=send_sem.at[at % FLIGHT], recv_sem=recv_sem.at[place],
            device_id=who, device_id_type=MESH))
        copies[-1].start()
        sizes.append(math.prod(dst.shape))

    def arrived(*names):
        for name in names:
            place, sizes = groups[name]
            tiles = sum(sizes) // (16 * 128)
            wide = max(k for k in range(1, K // 128 + 1) if tiles % k == 0)
            view = img.at[0:tiles // wide * 16, 0:wide * 128]
            pltpu.make_async_remote_copy(
                src_ref=view, dst_ref=view, send_sem=send_sem.at[0], recv_sem=recv_sem.at[place],
                device_id=sibling, device_id_type=MESH).wait_recv()

    whole, a_cols, b_cols = slice(0, K), slice(0, CUT), slice(CUT, K)

    def part(dx, dy, half, columns=whole, first=0, count=HALVES):
        return img.at[pl.ds(pl.multiple_of(BLOCK[dx, dy, half] * ROWS + c * HALVES + first, 16), count), columns]

    def own(half, columns=whole):
        return images.at[half * HALVES:(half + 1) * HALVES, columns]

    def share(group, blocks, *where):
        for block in blocks:
            at = part(*block, *where)
            send(group, at, at, sibling)

    for k in range(2):
        send(f"own_{k}", own(k), part(0, -1, k), up)
        send(f"own_{k}", own(1 - k), part(0, 1, 1 - k), down)
    for cols in (a_cols, b_cols):
        for k in range(2):
            send("own_1", own(k, cols), part(1, 0, k, cols), across)
    for k in range(2):
        send("s0", own(k), part(0, 0, k), sibling)
    get_expo.wait()
    give_expo = pltpu.make_async_remote_copy(
        src_ref=expo, dst_ref=expo_x, send_sem=expo_sem.at[0], recv_sem=expo_sem.at[1],
        device_id=across, device_id_type=MESH)
    give_expo.start()

    sub = lax.broadcasted_iota(jnp.int32, (16, 128), 0) % 2 == 0
    first_lanes = lax.broadcasted_iota(jnp.int32, (16, 128), 1) < HALVES

    def arrange(k, raw):
        turned = pltpu.roll(raw, HALVES, 1)
        even = jnp.where(first_lanes, raw, pltpu.roll(turned, 15, 0))
        odd = jnp.where(first_lanes, pltpu.roll(turned, 1, 0), raw)
        table[k] = jnp.where(sub, even, odd).astype(F32) * 0.25

    arrange(0, expo[...])
    get_partners.wait()
    own_row = lax.broadcasted_iota(jnp.int32, (6, 128), 0) * 128 + lax.broadcasted_iota(jnp.int32, (6, 128), 1)
    local = jnp.where(ref < 8, own_row, partners[...] - ((ref + 8) % 16) * R).astype(F32)
    lane = lax.broadcasted_iota(jnp.int32, (128, 128), 1)
    line = lax.broadcasted_iota(jnp.int32, (128, 128), 0).astype(F32)
    for i in range(R // 128):
        row = jnp.broadcast_to(local[i:i + 1, :], (128, 128))
        column = jnp.transpose(row)
        for j in range(R // 128):
            turn[j * 128:(j + 1) * 128, i * 128:(i + 1) * 128] = (row == line + j * 128.0).astype(F32).astype(BF16)
            place = lane + j * 128
            stands = place
            for rows in ORDERED:
                stands = jnp.where(place >= PLACE[rows.start], place - PLACE[rows.start] + rows.start, stands)
            pick[i * 128:(i + 1) * 128, j * 128:(j + 1) * 128] = (column == stands.astype(F32)).astype(F32).astype(BF16)

    put_pick = fetch(pick.at[:, 0:LATE], pick_late)
    get_refs.wait()

    @pl.loop(0, K // W)
    def _(j):
        cols = pl.ds(pl.multiple_of(j * W, W), W)
        refs[:, cols] = jnp.dot(turn[...], raw[:, cols], preferred_element_type=F32).astype(BF16)

    @pl.loop(0, R // 128)
    def _(i):
        block = refs[pl.ds(i * 128, 128), :].astype(F32)
        total = jnp.sum(block * block, axis=1, keepdims=True)
        norms[pl.ds(i * 128, 128), :] = jnp.broadcast_to(total * (0.5 / K), (128, UNIT))

    def product(rows, unit, columns):
        return lax.dot_general(refs[rows, columns], img[unit * UNIT:(unit + 1) * UNIT, columns],
                               (((1,), (1,)), ((), ())), preferred_element_type=F32)

    def scores(unit, column=0, begun=False):
        bias = jnp.concatenate([
            table[dx, pl.ds((((y + dy + 4) % 4) * 2 + (h if dx == 0 else 1 - h)) * 2 + half, 1), :]
            for dx, dy, half in UNITS[unit]], axis=1)

        @pl.loop(0, 2)
        def _(i):
            r = pl.ds(pl.multiple_of(i * (R // 2), R // 2), R // 2)
            if begun:
                s = early[r, :] + product(r, unit, a_cols)
            else:
                s = product(r, unit, whole)
            wts[r, column:column + UNIT] = jnp.exp(s * (1.0 / 64.0) - norms[r, :] - bias).astype(BF16)

    def column_of(dl, dz):
        return pl.ds(pl.multiple_of((((l + dl) % 2) * 4 + (z + dz) % 4) * W, W), W)

    def accumulate(unit, units=1, start=False, half=None):
        count = units * UNIT
        bounds = (0, 8) if half is None else (half * 4, half * 4 + 4)

        @pl.loop(*bounds)
        def _(j):
            added = jnp.dot(wts[:, 0:count], img[unit * UNIT:unit * UNIT + count, column_of(j // 4, j % 4)],
                            preferred_element_type=F32)
            acc[j] = added if start else acc[j] + added

    for copy in get_own:
        copy.wait()
    arrived("s0")
    scores(0)
    accumulate(0, start=True)

    arrived("own_0")
    share("s1", UNITS[1])
    send("far_b", part(0, -1, 0, b_cols), part(0, 2, 0, b_cols), up)
    send("far_b", part(0, 1, 1, b_cols), part(0, 2, 1, b_cols), down)
    send("x_5", part(0, -1, 0, b_cols), part(1, -1, 0, b_cols), across)
    send("x_5", part(0, 1, 1, b_cols), part(1, 1, 1, b_cols), across)
    send("far_a", part(0, -1, 0, a_cols), part(0, 2, 0, a_cols), up)
    send("far_a", part(0, 1, 1, a_cols), part(0, 2, 1, a_cols), down)
    arrived("s1")
    scores(1)
    accumulate(1)

    arrived("own_1")
    send("x_6", part(0, -1, 1, b_cols), part(1, -1, 1, b_cols), across)
    send("x_6", part(0, 1, 0, b_cols), part(1, 1, 0, b_cols), across)
    for k in range(2):
        send(f"y_{5 + k}", part(1, 0, k, a_cols), part(1, -1, k, a_cols), up)
        send(f"y_{5 + k}", part(1, 0, 1 - k, a_cols), part(1, 1, 1 - k, a_cols), down)
    share("s2", UNITS[2])
    share("s3", UNITS[3])
    give_expo.wait()
    arrange(1, expo_x[...])

    arrived("s2")
    scores(2)
    arrived("s3")
    scores(3, UNIT)
    accumulate(2, 2, half=0)
    arrived("far_b")
    for k in range(2):
        send("x_7", part(0, 2, k, b_cols), part(1, 2, k, b_cols), across)
    share("s4", UNITS[4], b_cols)
    arrived("x_5")
    share("s5", UNITS[5], b_cols)
    accumulate(2, 2, half=1)

    arrived("far_a")
    share("s4", UNITS[4], a_cols)
    arrived("s4")
    scores(4)
    accumulate(4, half=0)
    arrived("y_5")
    quarter = HALVES // 2
    for k in range(2):
        at = (a_cols, k * quarter, quarter)
        send(f"y_7{k}", part(1, -1, 0, *at), part(1, 2, 0, *at), up)
        send(f"y_7{k}", part(1, 1, 1, *at), part(1, 2, 1, *at), down)
    share("s5", UNITS[5], a_cols)
    accumulate(4, half=1)
    arrived("s5")
    scores(5)
    arrived("x_6")
    share("s6", UNITS[6], b_cols)
    accumulate(5, half=0)
    arrived("y_6")
    share("s6", UNITS[6], a_cols)
    accumulate(5, half=1)
    arrived("s6")
    scores(6)
    accumulate(6, half=0)
    arrived("x_7")
    share("s7b", UNITS[7], b_cols)
    arrived("y_70")
    share("s7a", UNITS[7], a_cols, 0, quarter)
    arrived("y_71")
    share("s7a", UNITS[7], a_cols, quarter, quarter)
    accumulate(6, half=1)
    arrived("s7b")

    @pl.loop(0, 2)
    def _(i):
        r = pl.ds(pl.multiple_of(i * (R // 2), R // 2), R // 2)
        early[r, :] = product(r, 7, b_cols)

    arrived("s7a")
    scores(7, begun=True)

    lo, hi = slice(0, HALF), slice(HALF, W)
    AB = slice(0, EARLY_ROWS.start), slice(EARLY_ROWS.stop, R)
    near = [slice(b.start - RA, b.stop - RA) for b in B_ROWS]

    def st_a(t, half, dl, a):
        return refs.at[a, pl.ds(pl.multiple_of(t * 1024 + half * W + dl * HALF, HALF), HALF)]

    def pair(t, half, a):
        return refs.at[a, t * 1024 + half * W:t * 1024 + half * W + W]

    def st_a2(k, a):
        return refs.at[a, 3072 + k * W:3072 + (k + 1) * W]

    def st_b(first, count, b):
        return refs.at[b, first:first + count]

    def a1(s):
        a = A_ROWS[s]
        send(f"a1{s}", pair(0, 0, a), r_a1.at[0, a, :], above)
        send(f"a1{s}", pair(0, 1, a), r_a1.at[1, a, :], below)

    def a2(s, up=True, down=True):
        if up:
            send(f"a2{s}", pair(1, 1, A_ROWS[s]), r_a2.at[0, A_ROWS[s], W:2 * W], above)
        if down:
            send(f"a2{s}", pair(2, 0, A_ROWS[s]), r_a2.at[1, A_ROWS[s], 0:W], below)

    def a2d(s):
        a = A_ROWS[s]
        arrived(f"a1{s}")
        for k, dz, cols, who in ((0, 1, lo, above), (1, 3, hi, below)):
            for dl in (1, 0):
                there = slice(dl * HALF, (dl + 1) * HALF)
                value = (acc[dl * 4 + dz, a, cols] + r_a1[k, a, there].astype(F32)).astype(BF16)
                refs[a, 3072 + k * W + dl * HALF:3072 + k * W + (dl + 1) * HALF] = value
            send(f"a2{s}", st_a2(k, a), r_a2.at[k, a, k * W:(k + 1) * W], who)

    def a3(s):
        a = A_ROWS[s]
        arrived(f"a2{s}")
        for dl in (1, 0):
            for half, cols in enumerate((lo, hi)):
                there = slice(half * W + dl * HALF, half * W + (dl + 1) * HALF)
                value = acc[dl * 4, a, cols] + r_a2[0, a, there].astype(F32) + r_a2[1, a, there].astype(F32)
                if dl:
                    wts[a, UNIT + half * HALF:UNIT + (half + 1) * HALF] = value.astype(BF16)
                else:
                    acc[0, a, cols] = value
            if dl:
                send(f"a3_{s}", wts.at[a, UNIT:UNIT + W], r_a3.at[a, :], beside)

    def b1(s, t):
        send(f"b1_{t}{s}" if t < 3 else f"b3{s}", st_b(t * W, W, B_ROWS[s]), r_b1.at[t, near[s], :], beside)

    def b2(s):
        b, n = B_ROWS[s], near[s]
        arrived(f"b1_0{s}")
        refs[b, 2048:2048 + W] = (acc[2, b, :] + r_b1[0, n, :].astype(F32)).astype(BF16)
        send(f"b2{s}", st_b(2048, HALF, b), r_b2.at[0, n, :], above)
        send(f"b2{s}", st_b(2048 + HALF, HALF, b), r_b2.at[1, n, :], below)

    def b3(s, k):
        b, n = B_ROWS[s], near[s]
        t, dz, cols, who = ((1, 1, hi, above), (2, 3, lo, below))[k]
        arrived(f"b1_{t}{s}")
        first = 2560 + k * HALF
        refs[b, first:first + HALF] = (acc[dz, b, cols] + r_b1[t, n, cols].astype(F32)).astype(BF16)
        send(f"b3{s}", st_b(first, HALF, b), r_b3.at[k, n, cols], who)

    def b3d(s):
        b, n = B_ROWS[s], near[s]
        arrived(f"b2{s}")
        for k, t, dz, cols, who in ((0, 1, 1, lo, above), (1, 2, 3, hi, below)):
            value = acc[dz, b, cols] + r_b1[t, n, cols].astype(F32) + r_b2[k, n, :].astype(F32)
            first = 3072 + k * HALF
            refs[b, first:first + HALF] = value.astype(BF16)
            send(f"b3{s}", st_b(first, HALF, b), r_b3.at[k, n, cols], who)

    def finish(name, rows):
        if name.endswith(str(LAST)):
            return
        final[rows, :] = acc[0, rows, :].astype(BF16)
        send(f"p1_{name}", final.at[rows, lo], relay.at[0, rows, :], up)
        send(f"p1_{name}", final.at[rows, hi], relay.at[1, rows, :], down)

    def finish_a(s):
        a = A_ROWS[s]
        arrived(f"a3_{s}")
        acc[0, a, :] = acc[0, a, :] + r_a3[a, :].astype(F32)
        finish(f"a{s}", a)

    def finish_b(s):
        b, n = B_ROWS[s], near[s]
        arrived(f"b3{s}")
        acc[0, b, :] = (acc[0, b, :] + r_b1[3, n, :].astype(F32)) + (r_b3[0, n, :].astype(F32) + r_b3[1, n, :].astype(F32))
        finish(f"b{s}", b)

    def pass_on(name, rows, s):
        arrived(f"p1_{name}")
        send(f"p2_{s}", relay.at[0, rows, :], other.at[rows, lo], up)
        send(f"p2_{s}", relay.at[1, rows, :], other.at[rows, hi], down)

    def settle(s):
        arrived(f"p2_{s}")
        for rows in (A_ROWS[s], B_ROWS[s]):
            value = acc[0, rows, :] + other[rows, :].astype(F32)
            at = slice(PLACE[rows.start], PLACE[rows.start] + rows.stop - rows.start)
            high[at, :] = value.astype(BF16)
            rest[at, :] = (value - value.astype(BF16).astype(F32)).astype(BF16)

    def order(s, k):
        r = slice(k * (R // 2), (k + 1) * (R // 2))
        at = slice(PLACE[A_ROWS[s].start], PLACE[B_ROWS[s].start] + B_ROWS[s].stop - B_ROWS[s].start)
        value = jnp.dot(pick[r, at], high[at, :], preferred_element_type=F32)
        value = value + jnp.dot(pick[r, at], rest[at, :], preferred_element_type=F32)
        acc[6, r, :] = value if s == 0 else acc[6, r, :] + value

    def c2(t):
        arrived(f"c1_{t}")
        send("c2", c_pass.at[t, 0], c_in.at[t, 0], up)
        send("c2", c_pass.at[t, 1], c_in.at[t, 1], down)

    def cin():
        arrived("c2")
        a, b = A_ROWS[LAST], B_ROWS[LAST]
        split = a.stop - a.start
        for t, dz in enumerate(ORDER):
            for dl in range(2):
                value = acc[dl * 4 + dz, EARLY_ROWS, :] + c_in[t, dl].astype(F32)
                acc[dl * 4 + dz, EARLY_ROWS, :] = value
                if t < 3:
                    for half, cols in enumerate((lo, hi)):
                        first = t * 1024 + half * W + dl * HALF
                        refs[a, first:first + HALF] = value[:split, cols].astype(BF16)
                if dl == 1:
                    refs[b, t * W:(t + 1) * W] = value[split:].astype(BF16)

    for t, dz in enumerate(ORDER):
        @pl.loop(0, 2)
        def _(i):
            dl = 1 - i
            added = jnp.dot(wts[:, 0:UNIT], img[7 * UNIT:8 * UNIT, column_of(dl, dz)], preferred_element_type=F32)
            value = acc[dl * 4 + dz] + added
            acc[dl * 4 + dz] = value
            c_out[t, dl] = value[EARLY_ROWS].astype(BF16)
            if t < 3:
                for half, cols in enumerate((lo, hi)):
                    st_a(t, half, dl, AB[0])[...] = value[AB[0], cols].astype(BF16)

            @pl.when(dl == 1)
            def _():
                refs[AB[1], t * W:(t + 1) * W] = value[AB[1]].astype(BF16)

        b1(0, t)
        send(f"c1_{t}", c_out.at[t, 0], c_pass.at[t, 0], up)
        send(f"c1_{t}", c_out.at[t, 1], c_pass.at[t, 1], down)
        if t == 0:
            a1(0)
        if t == 1:
            a2(0, down=False)
        if t == 2:
            a2(0, up=False)

    puts = []

    def give(k):
        r = slice(k * (R // 2), (k + 1) * (R // 2))
        return fetch(acc.at[6, r, :], sums.at[r, :])

    a2d(0)
    c2(0)
    b1(1, 1)
    b1(1, 0)
    c2(3)
    c2(2)
    b2(0)
    a1(1)
    a3(0)
    b1(1, 2)
    b3(0, 1)
    c2(1)
    b3(0, 0)
    b3d(0)
    b2(1)
    a2(1)
    a2d(1)
    cin()
    b1(2, 0)
    b1(1, 3)
    finish_b(0)
    finish_a(0)
    b3(1, 0)
    b3(1, 1)
    b3d(1)
    pass_on("b0", B_ROWS[0], 0)
    a3(1)
    b1(2, 1)
    b1(2, 2)
    a1(2)
    b2(2)
    pass_on("a0", A_ROWS[0], 0)
    a2(2)
    finish_b(1)
    a2d(2)
    finish_a(1)
    b1(2, 3)
    settle(0)
    pass_on("b1", B_ROWS[1], 1)
    order(0, 1)
    b3(2, 1)
    b3(2, 0)
    a3(2)
    pass_on("a1", A_ROWS[1], 1)
    b3d(2)
    order(0, 0)
    finish_b(2)
    finish_a(2)
    puts.append(fetch(acc.at[0, EARLY_ROWS, :], late))
    settle(1)
    order(1, 0)
    puts.append(give(0))
    order(1, 1)
    puts.append(give(1))
    for copy in copies[-FLIGHT:]:
        copy.wait_send()
    for copy in [put_pick] + puts:
        copy.wait()


PARTS = 4


def average(pick_hbm, late_hbm, sums_hbm, out_hbm, pick, late, sums, out, in_sem, out_sem):
    rows = [slice(i * (R // PARTS), (i + 1) * (R // PARTS)) for i in range(PARTS)]
    fetches = [pltpu.make_async_copy(late_hbm, late, in_sem.at[PARTS]),
               pltpu.make_async_copy(pick_hbm, pick, in_sem.at[PARTS + 1])]
    fetches += [pltpu.make_async_copy(sums_hbm.at[r, :], sums.at[r, :], in_sem.at[i]) for i, r in enumerate(rows)]
    for copy in fetches:
        copy.start()
    fetches[0].wait()
    fetches[1].wait()
    high = late[...].astype(BF16)
    rest = (late[...] - high.astype(F32)).astype(BF16)
    puts = []
    for i, r in enumerate(rows):
        added = jnp.dot(pick[r, :], high, preferred_element_type=F32) + jnp.dot(pick[r, :], rest, preferred_element_type=F32)
        fetches[2 + i].wait()
        out[r, :] = (sums[r, :] + added) * (0.5 / 128.0)
        puts.append(pltpu.make_async_copy(out.at[r, :], out_hbm.at[r, :], out_sem.at[i]))
        puts[-1].start()
    for copy in puts:
        copy.wait()


VMEM = 67043328


def body(images, exponents, references, partners):
    anywhere = pl.BlockSpec(memory_space=pl.ANY)
    sums, late, pick = pl.pallas_call(
        kernel,
        out_shape=(jax.ShapeDtypeStruct((R, W), F32), jax.ShapeDtypeStruct((LATE, W), F32),
                   jax.ShapeDtypeStruct((R, LATE), BF16)),
        in_specs=[anywhere] * 4,
        out_specs=(anywhere,) * 3,
        scratch_shapes=[
            pltpu.VMEM((8 * UNIT, K), BF16),
            pltpu.VMEM((R, K), BF16),
            pltpu.VMEM((R, K), BF16),
            pltpu.VMEM((8, R, W), F32),
            pltpu.VMEM((R, 3 * UNIT), BF16),
            pltpu.VMEM((R, UNIT), F32),
            pltpu.VMEM((R, R), BF16),
            pltpu.VMEM((R, R), BF16),
            pltpu.VMEM((16, 128), jnp.int32),
            pltpu.VMEM((16, 128), jnp.int32),
            pltpu.VMEM((2, 16, 128), F32),
            pltpu.VMEM((6, 128), jnp.int32),
            pltpu.VMEM((R, UNIT), F32),
            pltpu.VMEM((2, RA, W), BF16),
            pltpu.VMEM((2, RA, 2 * W), BF16),
            pltpu.VMEM((RA, W), BF16),
            pltpu.VMEM((4, RB, W), BF16),
            pltpu.VMEM((2, RB, HALF), BF16),
            pltpu.VMEM((2, RB, W), BF16),
            pltpu.VMEM((4, 2, LATE, W), BF16),
            pltpu.VMEM((4, 2, LATE, W), BF16),
            pltpu.VMEM((4, 2, LATE, W), BF16),
            pltpu.VMEM((R, W), BF16),
            pltpu.VMEM((2, R, HALF), BF16),
            pltpu.VMEM((R, W), BF16),
            pltpu.VMEM((R, W), BF16),
            pltpu.VMEM((R, W), BF16),
            pltpu.SemaphoreType.DMA((9,)),
            pltpu.SemaphoreType.DMA((FLIGHT,)),
            pltpu.SemaphoreType.DMA((GROUPS,)),
            pltpu.SemaphoreType.DMA((2,)),
        ],
        compiler_params=pltpu.CompilerParams(
            collective_id=0, has_side_effects=True, vmem_limit_bytes=VMEM),
    )(images, exponents.reshape(16, 128), references, partners.reshape(6, 128))
    return pl.pallas_call(
        average,
        out_shape=jax.ShapeDtypeStruct((R, W), F32),
        in_specs=[anywhere] * 3,
        out_specs=anywhere,
        scratch_shapes=[
            pltpu.VMEM((R, LATE), BF16),
            pltpu.VMEM((LATE, W), F32),
            pltpu.VMEM((R, W), F32),
            pltpu.VMEM((R, W), F32),
            pltpu.SemaphoreType.DMA((PARTS + 2,)),
            pltpu.SemaphoreType.DMA((PARTS,)),
        ],
        compiler_params=pltpu.CompilerParams(vmem_limit_bytes=67043328),
    )(pick, late, sums)


def solution(mesh):
    in_specs = (P(("img", "ref"), None), P("img"), P("ref", None), P("ref"))
    out_specs = P("ref", "img")
    return jax.shard_map(body, mesh=mesh, in_specs=in_specs, out_specs=out_specs, check_vma=False)
```

```python
import math

import jax
import jax.numpy as jnp
from jax import lax
from jax.experimental import pallas as pl
from jax.experimental.pallas import tpu as pltpu
from jax.sharding import PartitionSpec as P

MESH = pl.DeviceIdType.MESH
F32 = jnp.float32
BF16 = jnp.bfloat16

R = 768
K = 4096
W = 512
ROWS = 128
UNIT = 256
CUT = 2304
RA = 416
RB = R - RA
HALF = W // 2
A_ROWS = (slice(0, 240), slice(240, 352), slice(352, 416))
B_ROWS = (slice(624, 768), slice(480, 624), slice(416, 480))
LAST = len(A_ROWS) - 1
EARLY_ROWS = slice(A_ROWS[LAST].start, B_ROWS[LAST].stop)
LATE = EARLY_ROWS.stop - EARLY_ROWS.start
ORDERED = [rows for s in (2, 1, 0) for rows in (A_ROWS[s], B_ROWS[s])]
PLACE = {}
for rows in ORDERED:
    PLACE[rows.start] = sum(rows.stop - rows.start for rows in ORDERED[:len(PLACE)])
HALVES = ROWS // 2
FLIGHT = 32
GROUPS = 60

UNITS = (
    ((0, 0, 0), (0, 0, 1)),
    ((0, 1, 1), (0, -1, 0)),
    ((1, 0, 0), (1, 0, 1)),
    ((0, 1, 0), (0, -1, 1)),
    ((0, 2, 0), (0, 2, 1)),
    ((1, 1, 1), (1, -1, 0)),
    ((1, 1, 0), (1, -1, 1)),
    ((1, 2, 0), (1, 2, 1)),
)
BLOCK = {block: i for i, block in enumerate(block for unit in UNITS for block in unit)}
ORDER = (2, 1, 3, 0)


def kernel(images, expo_hbm, refs_hbm, partners_hbm, sums, late, pick_late, img, raw, refs, acc, wts, norms, pick, turn,
           expo, expo_x, table, partners, early, r_a1, r_a2, r_a3, r_b1, r_b2, r_b3,
           c_out, c_pass, c_in, final, relay, other, high, rest, local_sem, send_sem, recv_sem, expo_sem):
    ref, im = lax.axis_index("ref"), lax.axis_index("img")
    y, h, c = ref // 4, (ref // 2) % 2, ref % 2
    l, z = im // 4, im % 4

    def device(y, h, c, l, z):
        return {"ref": y * 4 + h * 2 + c, "img": l * 4 + z}

    up = device((y + 1) % 4, h, c, l, z)
    down = device((y + 3) % 4, h, c, l, z)
    across = device(y, 1 - h, c, 1 - l, z)
    sibling = device(y, h, 1 - c, l, z)
    beside = device(y, h, c, 1 - l, z)
    above = device(y, h, c, l, (z + 1) % 4)
    below = device(y, h, c, l, (z + 3) % 4)

    started = []

    def fetch(src, dst):
        started.append(pltpu.make_async_copy(src, dst, local_sem.at[len(started)]))
        started[-1].start()
        return started[-1]

    get_expo = fetch(expo_hbm, expo)
    get_partners = fetch(partners_hbm, partners)
    get_refs = fetch(refs_hbm, raw)
    get_own = [fetch(images.at[k * HALVES:(k + 1) * HALVES, :],
                     img.at[pl.ds(pl.multiple_of(k * ROWS + c * HALVES, HALVES), HALVES), :]) for k in range(2)]

    neighbours = (up, down, across, sibling, beside, above, below)
    barrier = pltpu.get_barrier_semaphore()
    for who in neighbours:
        pl.semaphore_signal(barrier, inc=1, device_id=who, device_id_type=MESH)
    pl.semaphore_wait(barrier, len(neighbours))

    copies, groups = [], {}

    def send(group, src, dst, who):
        at = len(copies)
        if at >= FLIGHT:
            copies[at - FLIGHT].wait_send()
        place, sizes = groups.setdefault(group, (len(groups), []))
        copies.append(pltpu.make_async_remote_copy(
            src_ref=src, dst_ref=dst, send_sem=send_sem.at[at % FLIGHT], recv_sem=recv_sem.at[place],
            device_id=who, device_id_type=MESH))
        copies[-1].start()
        sizes.append(math.prod(dst.shape))

    def arrived(*names):
        for name in names:
            place, sizes = groups[name]
            tiles = sum(sizes) // (16 * 128)
            wide = max(k for k in range(1, K // 128 + 1) if tiles % k == 0)
            view = img.at[0:tiles // wide * 16, 0:wide * 128]
            pltpu.make_async_remote_copy(
                src_ref=view, dst_ref=view, send_sem=send_sem.at[0], recv_sem=recv_sem.at[place],
                device_id=sibling, device_id_type=MESH).wait_recv()

    whole, a_cols, b_cols = slice(0, K), slice(0, CUT), slice(CUT, K)

    def part(dx, dy, half, columns=whole, first=0, count=HALVES):
        return img.at[pl.ds(pl.multiple_of(BLOCK[dx, dy, half] * ROWS + c * HALVES + first, 16), count), columns]

    def own(half, columns=whole):
        return images.at[half * HALVES:(half + 1) * HALVES, columns]

    def share(group, blocks, *where):
        for block in blocks:
            at = part(*block, *where)
            send(group, at, at, sibling)

    for k in range(2):
        send(f"own_{k}", own(k), part(0, -1, k), up)
        send(f"own_{k}", own(1 - k), part(0, 1, 1 - k), down)
    for cols in (a_cols, b_cols):
        for k in range(2):
            send("own_1", own(k, cols), part(1, 0, k, cols), across)
    for k in range(2):
        send("s0", own(k), part(0, 0, k), sibling)
    get_expo.wait()
    give_expo = pltpu.make_async_remote_copy(
        src_ref=expo, dst_ref=expo_x, send_sem=expo_sem.at[0], recv_sem=expo_sem.at[1],
        device_id=across, device_id_type=MESH)
    give_expo.start()

    sub = lax.broadcasted_iota(jnp.int32, (16, 128), 0) % 2 == 0
    first_lanes = lax.broadcasted_iota(jnp.int32, (16, 128), 1) < HALVES

    def arrange(k, raw):
        turned = pltpu.roll(raw, HALVES, 1)
        even = jnp.where(first_lanes, raw, pltpu.roll(turned, 15, 0))
        odd = jnp.where(first_lanes, pltpu.roll(turned, 1, 0), raw)
        table[k] = jnp.where(sub, even, odd).astype(F32) * 0.25

    arrange(0, expo[...])
    get_partners.wait()
    own_row = lax.broadcasted_iota(jnp.int32, (6, 128), 0) * 128 + lax.broadcasted_iota(jnp.int32, (6, 128), 1)
    local = jnp.where(ref < 8, own_row, partners[...] - ((ref + 8) % 16) * R).astype(F32)
    lane = lax.broadcasted_iota(jnp.int32, (128, 128), 1)
    line = lax.broadcasted_iota(jnp.int32, (128, 128), 0).astype(F32)
    for i in range(R // 128):
        row = jnp.broadcast_to(local[i:i + 1, :], (128, 128))
        column = jnp.transpose(row)
        for j in range(R // 128):
            turn[j * 128:(j + 1) * 128, i * 128:(i + 1) * 128] = (row == line + j * 128.0).astype(F32).astype(BF16)
            place = lane + j * 128
            stands = place
            for rows in ORDERED:
                stands = jnp.where(place >= PLACE[rows.start], place - PLACE[rows.start] + rows.start, stands)
            pick[i * 128:(i + 1) * 128, j * 128:(j + 1) * 128] = (column == stands.astype(F32)).astype(F32).astype(BF16)

    put_pick = fetch(pick.at[:, 0:LATE], pick_late)
    get_refs.wait()

    @pl.loop(0, K // W)
    def _(j):
        cols = pl.ds(pl.multiple_of(j * W, W), W)
        refs[:, cols] = jnp.dot(turn[...], raw[:, cols], preferred_element_type=F32).astype(BF16)

    @pl.loop(0, R // 128)
    def _(i):
        block = refs[pl.ds(i * 128, 128), :].astype(F32)
        total = jnp.sum(block * block, axis=1, keepdims=True)
        norms[pl.ds(i * 128, 128), :] = jnp.broadcast_to(total * (0.5 / K), (128, UNIT))

    def product(rows, unit, columns):
        return lax.dot_general(refs[rows, columns], img[unit * UNIT:(unit + 1) * UNIT, columns],
                               (((1,), (1,)), ((), ())), preferred_element_type=F32)

    def scores(unit, column=0, begun=False):
        bias = jnp.concatenate([
            table[dx, pl.ds((((y + dy + 4) % 4) * 2 + (h if dx == 0 else 1 - h)) * 2 + half, 1), :]
            for dx, dy, half in UNITS[unit]], axis=1)

        @pl.loop(0, 2)
        def _(i):
            r = pl.ds(pl.multiple_of(i * (R // 2), R // 2), R // 2)
            if begun:
                s = early[r, :] + product(r, unit, a_cols)
            else:
                s = product(r, unit, whole)
            wts[r, column:column + UNIT] = jnp.exp(s * (1.0 / 64.0) - norms[r, :] - bias).astype(BF16)

    def column_of(dl, dz):
        return pl.ds(pl.multiple_of((((l + dl) % 2) * 4 + (z + dz) % 4) * W, W), W)

    def accumulate(unit, units=1, start=False, bounds=(0, 8)):
        count = units * UNIT

        @pl.loop(*bounds)
        def _(j):
            added = jnp.dot(wts[:, 0:count], img[unit * UNIT:unit * UNIT + count, column_of(j // 4, j % 4)],
                            preferred_element_type=F32)
            acc[j] = added if start else acc[j] + added

    for copy in get_own:
        copy.wait()
    arrived("s0")
    scores(0)
    accumulate(0, start=True)

    arrived("own_0")
    share("s1", UNITS[1])
    send("far_b", part(0, -1, 0, b_cols), part(0, 2, 0, b_cols), up)
    send("far_b", part(0, 1, 1, b_cols), part(0, 2, 1, b_cols), down)
    send("x_5", part(0, -1, 0, b_cols), part(1, -1, 0, b_cols), across)
    send("x_5", part(0, 1, 1, b_cols), part(1, 1, 1, b_cols), across)
    send("far_a", part(0, -1, 0, a_cols), part(0, 2, 0, a_cols), up)
    send("far_a", part(0, 1, 1, a_cols), part(0, 2, 1, a_cols), down)
    arrived("s1")
    scores(1)
    accumulate(1)

    arrived("own_1")
    send("x_6", part(0, -1, 1, b_cols), part(1, -1, 1, b_cols), across)
    send("x_6", part(0, 1, 0, b_cols), part(1, 1, 0, b_cols), across)
    for k in range(2):
        send(f"y_{5 + k}", part(1, 0, k, a_cols), part(1, -1, k, a_cols), up)
        send(f"y_{5 + k}", part(1, 0, 1 - k, a_cols), part(1, 1, 1 - k, a_cols), down)
    share("s2", UNITS[2])
    share("s3", UNITS[3])
    give_expo.wait()
    arrange(1, expo_x[...])

    arrived("s2")
    scores(2)
    arrived("s3")
    scores(3, UNIT)
    accumulate(2, 2, bounds=(0, 4))
    arrived("far_b")
    quarter = HALVES // 2
    for k in range(4):
        at = (k // 2, b_cols, k % 2 * quarter, quarter)
        send("x_70" if k < 3 else "x_71", part(0, 2, *at), part(1, 2, *at), across)
    share("s4", UNITS[4], b_cols)
    arrived("x_5")
    share("s5", UNITS[5], b_cols)
    accumulate(2, 2, bounds=(4, 6))

    arrived("far_a")
    share("s4", UNITS[4], a_cols)
    accumulate(2, 2, bounds=(6, 8))
    arrived("s4")
    scores(4)
    accumulate(4, bounds=(0, 4))
    arrived("y_5")
    for k in range(2):
        at = (a_cols, k * quarter, quarter)
        send(f"y_7{k}", part(1, -1, 0, *at), part(1, 2, 0, *at), up)
        send(f"y_7{k}", part(1, 1, 1, *at), part(1, 2, 1, *at), down)
    share("s5", UNITS[5], a_cols)
    accumulate(4, bounds=(4, 8))
    arrived("s5")
    scores(5)
    arrived("x_6")
    share("s6b", UNITS[6], b_cols)
    accumulate(5, bounds=(0, 4))
    arrived("s6b")

    @pl.loop(0, 2)
    def _(i):
        r = pl.ds(pl.multiple_of(i * (R // 2), R // 2), R // 2)
        early[r, :] = product(r, 6, b_cols)

    arrived("y_6")
    share("s6a", UNITS[6], a_cols)
    accumulate(5, bounds=(4, 8))
    arrived("s6a")
    scores(6, begun=True)
    accumulate(6, bounds=(0, 4))
    arrived("y_70")
    share("s7", UNITS[7], a_cols, 0, quarter)
    arrived("x_70")
    share("s7", UNITS[7], b_cols, 0, quarter)
    share("s7", UNITS[7][:1], b_cols, quarter, quarter)
    accumulate(6, bounds=(4, 6))
    arrived("x_71")
    share("s7", UNITS[7][1:], b_cols, quarter, quarter)
    arrived("y_71")
    share("s7", UNITS[7], a_cols, quarter, quarter)
    accumulate(6, bounds=(6, 8))
    arrived("s7")
    scores(7)

    lo, hi = slice(0, HALF), slice(HALF, W)
    AB = slice(0, EARLY_ROWS.start), slice(EARLY_ROWS.stop, R)
    near = [slice(b.start - RA, b.stop - RA) for b in B_ROWS]

    def st_a(t, half, dl, a):
        return refs.at[a, pl.ds(pl.multiple_of(t * 1024 + half * W + dl * HALF, HALF), HALF)]

    def pair(t, half, a):
        return refs.at[a, t * 1024 + half * W:t * 1024 + half * W + W]

    def st_a2(k, a):
        return refs.at[a, 3072 + k * W:3072 + (k + 1) * W]

    def st_b(first, count, b):
        return refs.at[b, first:first + count]

    def a1(s):
        a = A_ROWS[s]
        send(f"a1{s}", pair(0, 0, a), r_a1.at[0, a, :], above)
        send(f"a1{s}", pair(0, 1, a), r_a1.at[1, a, :], below)

    def a2(s, up=True, down=True):
        if up:
            send(f"a2{s}", pair(1, 1, A_ROWS[s]), r_a2.at[0, A_ROWS[s], W:2 * W], above)
        if down:
            send(f"a2{s}", pair(2, 0, A_ROWS[s]), r_a2.at[1, A_ROWS[s], 0:W], below)

    def a2d(s):
        a = A_ROWS[s]
        arrived(f"a1{s}")
        for k, dz, cols, who in ((0, 1, lo, above), (1, 3, hi, below)):
            for dl in (1, 0):
                there = slice(dl * HALF, (dl + 1) * HALF)
                value = (acc[dl * 4 + dz, a, cols] + r_a1[k, a, there].astype(F32)).astype(BF16)
                refs[a, 3072 + k * W + dl * HALF:3072 + k * W + (dl + 1) * HALF] = value
            send(f"a2{s}", st_a2(k, a), r_a2.at[k, a, k * W:(k + 1) * W], who)

    def a3(s):
        a = A_ROWS[s]
        arrived(f"a2{s}")
        for dl in (1, 0):
            for half, cols in enumerate((lo, hi)):
                there = slice(half * W + dl * HALF, half * W + (dl + 1) * HALF)
                value = acc[dl * 4, a, cols] + r_a2[0, a, there].astype(F32) + r_a2[1, a, there].astype(F32)
                if dl:
                    wts[a, UNIT + half * HALF:UNIT + (half + 1) * HALF] = value.astype(BF16)
                else:
                    acc[0, a, cols] = value
            if dl:
                send(f"a3_{s}", wts.at[a, UNIT:UNIT + W], r_a3.at[a, :], beside)

    def b1(s, t):
        send(f"b1_{t}{s}" if t < 3 else f"b3{s}", st_b(t * W, W, B_ROWS[s]), r_b1.at[t, near[s], :], beside)

    def b2(s):
        b, n = B_ROWS[s], near[s]
        arrived(f"b1_0{s}")
        refs[b, 2048:2048 + W] = (acc[2, b, :] + r_b1[0, n, :].astype(F32)).astype(BF16)
        send(f"b2{s}", st_b(2048, HALF, b), r_b2.at[0, n, :], above)
        send(f"b2{s}", st_b(2048 + HALF, HALF, b), r_b2.at[1, n, :], below)

    def b3(s, k):
        b, n = B_ROWS[s], near[s]
        t, dz, cols, who = ((1, 1, hi, above), (2, 3, lo, below))[k]
        arrived(f"b1_{t}{s}")
        first = 2560 + k * HALF
        refs[b, first:first + HALF] = (acc[dz, b, cols] + r_b1[t, n, cols].astype(F32)).astype(BF16)
        send(f"b3{s}", st_b(first, HALF, b), r_b3.at[k, n, cols], who)

    def b3d(s):
        b, n = B_ROWS[s], near[s]
        arrived(f"b2{s}")
        for k, t, dz, cols, who in ((0, 1, 1, lo, above), (1, 2, 3, hi, below)):
            value = acc[dz, b, cols] + r_b1[t, n, cols].astype(F32) + r_b2[k, n, :].astype(F32)
            first = 3072 + k * HALF
            refs[b, first:first + HALF] = value.astype(BF16)
            send(f"b3{s}", st_b(first, HALF, b), r_b3.at[k, n, cols], who)

    def finish(name, rows):
        if name.endswith(str(LAST)):
            return
        final[rows, :] = acc[0, rows, :].astype(BF16)
        send(f"p1_{name}", final.at[rows, lo], relay.at[0, rows, :], up)
        send(f"p1_{name}", final.at[rows, hi], relay.at[1, rows, :], down)

    def finish_a(s):
        a = A_ROWS[s]
        arrived(f"a3_{s}")
        acc[0, a, :] = acc[0, a, :] + r_a3[a, :].astype(F32)
        finish(f"a{s}", a)

    def finish_b(s):
        b, n = B_ROWS[s], near[s]
        arrived(f"b3{s}")
        acc[0, b, :] = (acc[0, b, :] + r_b1[3, n, :].astype(F32)) + (r_b3[0, n, :].astype(F32) + r_b3[1, n, :].astype(F32))
        finish(f"b{s}", b)

    def pass_on(name, rows, s):
        arrived(f"p1_{name}")
        send(f"p2_{s}", relay.at[0, rows, :], other.at[rows, lo], up)
        send(f"p2_{s}", relay.at[1, rows, :], other.at[rows, hi], down)

    def settle(s):
        arrived(f"p2_{s}")
        for rows in (A_ROWS[s], B_ROWS[s]):
            value = acc[0, rows, :] + other[rows, :].astype(F32)
            at = slice(PLACE[rows.start], PLACE[rows.start] + rows.stop - rows.start)
            high[at, :] = value.astype(BF16)
            rest[at, :] = (value - value.astype(BF16).astype(F32)).astype(BF16)

    def order(s, k):
        r = slice(k * (R // 2), (k + 1) * (R // 2))
        at = slice(PLACE[A_ROWS[s].start], PLACE[B_ROWS[s].start] + B_ROWS[s].stop - B_ROWS[s].start)
        value = jnp.dot(pick[r, at], high[at, :], preferred_element_type=F32)
        value = value + jnp.dot(pick[r, at], rest[at, :], preferred_element_type=F32)
        acc[6, r, :] = value if s == 0 else acc[6, r, :] + value

    def c2(t):
        arrived(f"c1_{t}")
        send("c2", c_pass.at[t, 0], c_in.at[t, 0], up)
        send("c2", c_pass.at[t, 1], c_in.at[t, 1], down)

    def cin():
        arrived("c2")
        a, b = A_ROWS[LAST], B_ROWS[LAST]
        split = a.stop - a.start
        for t, dz in enumerate(ORDER):
            for dl in range(2):
                value = acc[dl * 4 + dz, EARLY_ROWS, :] + c_in[t, dl].astype(F32)
                acc[dl * 4 + dz, EARLY_ROWS, :] = value
                if t < 3:
                    for half, cols in enumerate((lo, hi)):
                        first = t * 1024 + half * W + dl * HALF
                        refs[a, first:first + HALF] = value[:split, cols].astype(BF16)
                if dl == 1:
                    refs[b, t * W:(t + 1) * W] = value[split:].astype(BF16)

    def last_unit(t, dl):
        dz = ORDER[t]
        added = jnp.dot(wts[:, 0:UNIT], img[7 * UNIT:8 * UNIT, column_of(dl, dz)], preferred_element_type=F32)
        value = acc[dl * 4 + dz] + added
        acc[dl * 4 + dz] = value
        c_out[t, dl] = value[EARLY_ROWS].astype(BF16)
        if t < 3:
            for half, cols in enumerate((lo, hi)):
                st_a(t, half, dl, AB[0])[...] = value[AB[0], cols].astype(BF16)
        return value

    for dl in (1, 0):
        value = last_unit(0, dl)
        if dl == 1:
            refs[AB[1], 0:W] = value[AB[1]].astype(BF16)
            b1(0, 0)
        a = A_ROWS[0]
        for half, who in ((0, above), (1, below)):
            first = half * W + dl * HALF
            send("a10", refs.at[a, first:first + HALF], r_a1.at[half, a, dl * HALF:(dl + 1) * HALF], who)
        send("c1_0", c_out.at[0, dl], c_pass.at[0, dl], down if dl else up)

    for t in range(1, 4):
        @pl.loop(0, 2)
        def _(i):
            dl = 1 - i
            value = last_unit(t, dl)

            @pl.when(dl == 1)
            def _():
                refs[AB[1], t * W:(t + 1) * W] = value[AB[1]].astype(BF16)

        b1(0, t)
        if t == 1:
            a2(0, down=False)
        if t == 2:
            a2(0, up=False)
        send(f"c1_{t}", c_out.at[t, 0], c_pass.at[t, 0], up)
        send(f"c1_{t}", c_out.at[t, 1], c_pass.at[t, 1], down)

    puts = []

    def give(k):
        r = slice(k * (R // 2), (k + 1) * (R // 2))
        return fetch(acc.at[6, r, :], sums.at[r, :])

    a2d(0)
    c2(0)
    b1(1, 1)
    b1(1, 0)
    c2(3)
    c2(2)
    b2(0)
    a1(1)
    a3(0)
    b1(1, 2)
    b3(0, 1)
    c2(1)
    b3(0, 0)
    b3d(0)
    b2(1)
    a2(1)
    a2d(1)
    cin()
    b1(2, 0)
    b1(1, 3)
    finish_b(0)
    finish_a(0)
    b3(1, 0)
    b3(1, 1)
    b3d(1)
    pass_on("b0", B_ROWS[0], 0)
    a3(1)
    b1(2, 1)
    b1(2, 2)
    a1(2)
    b2(2)
    pass_on("a0", A_ROWS[0], 0)
    a2(2)
    finish_b(1)
    a2d(2)
    finish_a(1)
    b1(2, 3)
    settle(0)
    pass_on("b1", B_ROWS[1], 1)
    order(0, 1)
    b3(2, 1)
    b3(2, 0)
    a3(2)
    pass_on("a1", A_ROWS[1], 1)
    b3d(2)
    order(0, 0)
    finish_b(2)
    finish_a(2)
    puts.append(fetch(acc.at[0, EARLY_ROWS, :], late))
    settle(1)
    order(1, 0)
    puts.append(give(0))
    order(1, 1)
    puts.append(give(1))
    for copy in copies[-FLIGHT:]:
        copy.wait_send()
    for copy in [put_pick] + puts:
        copy.wait()


PARTS = 4


def average(pick_hbm, late_hbm, sums_hbm, out_hbm, pick, late, sums, out, in_sem, out_sem):
    rows = [slice(i * (R // PARTS), (i + 1) * (R // PARTS)) for i in range(PARTS)]
    fetches = [pltpu.make_async_copy(late_hbm, late, in_sem.at[PARTS]),
               pltpu.make_async_copy(pick_hbm, pick, in_sem.at[PARTS + 1])]
    fetches += [pltpu.make_async_copy(sums_hbm.at[r, :], sums.at[r, :], in_sem.at[i]) for i, r in enumerate(rows)]
    for copy in fetches:
        copy.start()
    fetches[0].wait()
    fetches[1].wait()
    high = late[...].astype(BF16)
    rest = (late[...] - high.astype(F32)).astype(BF16)
    puts = []
    for i, r in enumerate(rows):
        added = jnp.dot(pick[r, :], high, preferred_element_type=F32) + jnp.dot(pick[r, :], rest, preferred_element_type=F32)
        fetches[2 + i].wait()
        out[r, :] = (sums[r, :] + added) * (0.5 / 128.0)
        puts.append(pltpu.make_async_copy(out.at[r, :], out_hbm.at[r, :], out_sem.at[i]))
        puts[-1].start()
    for copy in puts:
        copy.wait()


VMEM = 67043328


def body(images, exponents, references, partners):
    anywhere = pl.BlockSpec(memory_space=pl.ANY)
    sums, late, pick = pl.pallas_call(
        kernel,
        out_shape=(jax.ShapeDtypeStruct((R, W), F32), jax.ShapeDtypeStruct((LATE, W), F32),
                   jax.ShapeDtypeStruct((R, LATE), BF16)),
        in_specs=[anywhere] * 4,
        out_specs=(anywhere,) * 3,
        scratch_shapes=[
            pltpu.VMEM((8 * UNIT, K), BF16),
            pltpu.VMEM((R, K), BF16),
            pltpu.VMEM((R, K), BF16),
            pltpu.VMEM((8, R, W), F32),
            pltpu.VMEM((R, 3 * UNIT), BF16),
            pltpu.VMEM((R, UNIT), F32),
            pltpu.VMEM((R, R), BF16),
            pltpu.VMEM((R, R), BF16),
            pltpu.VMEM((16, 128), jnp.int32),
            pltpu.VMEM((16, 128), jnp.int32),
            pltpu.VMEM((2, 16, 128), F32),
            pltpu.VMEM((6, 128), jnp.int32),
            pltpu.VMEM((R, UNIT), F32),
            pltpu.VMEM((2, RA, W), BF16),
            pltpu.VMEM((2, RA, 2 * W), BF16),
            pltpu.VMEM((RA, W), BF16),
            pltpu.VMEM((4, RB, W), BF16),
            pltpu.VMEM((2, RB, HALF), BF16),
            pltpu.VMEM((2, RB, W), BF16),
            pltpu.VMEM((4, 2, LATE, W), BF16),
            pltpu.VMEM((4, 2, LATE, W), BF16),
            pltpu.VMEM((4, 2, LATE, W), BF16),
            pltpu.VMEM((R, W), BF16),
            pltpu.VMEM((2, R, HALF), BF16),
            pltpu.VMEM((R, W), BF16),
            pltpu.VMEM((R, W), BF16),
            pltpu.VMEM((R, W), BF16),
            pltpu.SemaphoreType.DMA((9,)),
            pltpu.SemaphoreType.DMA((FLIGHT,)),
            pltpu.SemaphoreType.DMA((GROUPS,)),
            pltpu.SemaphoreType.DMA((2,)),
        ],
        compiler_params=pltpu.CompilerParams(
            collective_id=0, has_side_effects=True, vmem_limit_bytes=VMEM),
    )(images, exponents.reshape(16, 128), references, partners.reshape(6, 128))
    return pl.pallas_call(
        average,
        out_shape=jax.ShapeDtypeStruct((R, W), F32),
        in_specs=[anywhere] * 3,
        out_specs=anywhere,
        scratch_shapes=[
            pltpu.VMEM((R, LATE), BF16),
            pltpu.VMEM((LATE, W), F32),
            pltpu.VMEM((R, W), F32),
            pltpu.VMEM((R, W), F32),
            pltpu.SemaphoreType.DMA((PARTS + 2,)),
            pltpu.SemaphoreType.DMA((PARTS,)),
        ],
        compiler_params=pltpu.CompilerParams(vmem_limit_bytes=67043328),
    )(pick, late, sums)


def solution(mesh):
    in_specs = (P(("img", "ref"), None), P("img"), P("ref", None), P("ref"))
    out_specs = P("ref", "img")
    return jax.shard_map(body, mesh=mesh, in_specs=in_specs, out_specs=out_specs, check_vma=False)
```

```python
import math

import jax
import jax.numpy as jnp
from jax import lax
from jax.experimental import pallas as pl
from jax.experimental.pallas import tpu as pltpu
from jax.sharding import PartitionSpec as P

MESH = pl.DeviceIdType.MESH
F32 = jnp.float32
BF16 = jnp.bfloat16

R = 768
K = 4096
W = 512
ROWS = 128
UNIT = 256
CUT = 2304
RA = 416
RB = R - RA
HALF = W // 2
A_ROWS = (slice(0, 240), slice(240, 352), slice(352, 416))
B_ROWS = (slice(624, 768), slice(480, 624), slice(416, 480))
LAST = len(A_ROWS) - 1
EARLY_ROWS = slice(A_ROWS[LAST].start, B_ROWS[LAST].stop)
LATE = EARLY_ROWS.stop - EARLY_ROWS.start
ORDERED = [rows for s in (2, 1, 0) for rows in (A_ROWS[s], B_ROWS[s])]
PLACE = {}
for rows in ORDERED:
    PLACE[rows.start] = sum(rows.stop - rows.start for rows in ORDERED[:len(PLACE)])
HALVES = ROWS // 2
FLIGHT = 24
GROUPS = 56

UNITS = (
    ((0, 0, 0), (0, 0, 1)),
    ((0, 1, 1), (0, -1, 0)),
    ((1, 0, 0), (1, 0, 1)),
    ((0, 1, 0), (0, -1, 1)),
    ((0, 2, 0), (0, 2, 1)),
    ((1, 1, 1), (1, -1, 0)),
    ((1, 1, 0), (1, -1, 1)),
    ((1, 2, 0), (1, 2, 1)),
)
BLOCK = {block: i for i, block in enumerate(block for unit in UNITS for block in unit)}
ORDER = (2, 1, 3, 0)


def kernel(images, expo_hbm, refs_hbm, partners_hbm, sums, late, pick_late, img, raw, refs, acc, wts, norms, pick, turn,
           expo, expo_x, table, partners, early, r_a1, r_a2, r_a3, r_b1, r_b2, r_b3,
           c_out, c_pass, c_in, final, relay, other, high, rest, local_sem, send_sem, recv_sem, expo_sem):
    ref, im = lax.axis_index("ref"), lax.axis_index("img")
    y, h, c = ref // 4, (ref // 2) % 2, ref % 2
    l, z = im // 4, im % 4

    def device(y, h, c, l, z):
        return {"ref": y * 4 + h * 2 + c, "img": l * 4 + z}

    up = device((y + 1) % 4, h, c, l, z)
    down = device((y + 3) % 4, h, c, l, z)
    across = device(y, 1 - h, c, 1 - l, z)
    sibling = device(y, h, 1 - c, l, z)
    beside = device(y, h, c, 1 - l, z)
    above = device(y, h, c, l, (z + 1) % 4)
    below = device(y, h, c, l, (z + 3) % 4)

    started = []

    def fetch(src, dst):
        started.append(pltpu.make_async_copy(src, dst, local_sem.at[len(started)]))
        started[-1].start()
        return started[-1]

    get_expo = fetch(expo_hbm, expo)
    get_partners = fetch(partners_hbm, partners)
    get_refs = fetch(refs_hbm, raw)
    get_own = [fetch(images.at[k * HALVES:(k + 1) * HALVES, :],
                     img.at[pl.ds(pl.multiple_of(k * ROWS + c * HALVES, HALVES), HALVES), :]) for k in range(2)]

    neighbours = (up, down, across, sibling, beside, above, below)
    barrier = pltpu.get_barrier_semaphore()
    for who in neighbours:
        pl.semaphore_signal(barrier, inc=1, device_id=who, device_id_type=MESH)
    pl.semaphore_wait(barrier, len(neighbours))

    copies, groups = [], {}

    def send(group, src, dst, who):
        at = len(copies)
        if at >= FLIGHT:
            copies[at - FLIGHT].wait_send()
        place, sizes = groups.setdefault(group, (len(groups), []))
        copies.append(pltpu.make_async_remote_copy(
            src_ref=src, dst_ref=dst, send_sem=send_sem.at[at % FLIGHT], recv_sem=recv_sem.at[place],
            device_id=who, device_id_type=MESH))
        copies[-1].start()
        sizes.append(math.prod(dst.shape))

    def arrived(*names):
        for name in names:
            place, sizes = groups[name]
            tiles = sum(sizes) // (16 * 128)
            wide = max(k for k in range(1, K // 128 + 1) if tiles % k == 0)
            view = img.at[0:tiles // wide * 16, 0:wide * 128]
            pltpu.make_async_remote_copy(
                src_ref=view, dst_ref=view, send_sem=send_sem.at[0], recv_sem=recv_sem.at[place],
                device_id=sibling, device_id_type=MESH).wait_recv()

    whole, a_cols, b_cols = slice(0, K), slice(0, CUT), slice(CUT, K)

    def part(dx, dy, half, columns=whole, first=0, count=HALVES):
        return img.at[pl.ds(pl.multiple_of(BLOCK[dx, dy, half] * ROWS + c * HALVES + first, 16), count), columns]

    def own(half, columns=whole):
        return images.at[half * HALVES:(half + 1) * HALVES, columns]

    def share(group, blocks, *where):
        for block in blocks:
            at = part(*block, *where)
            send(group, at, at, sibling)

    for k in range(2):
        send(f"own_{k}", own(k), part(0, -1, k), up)
        send(f"own_{k}", own(1 - k), part(0, 1, 1 - k), down)
    for cols in (a_cols, b_cols):
        for k in range(2):
            send("own_1", own(k, cols), part(1, 0, k, cols), across)
    for k in range(2):
        send("s0", own(k), part(0, 0, k), sibling)
    get_expo.wait()
    give_expo = pltpu.make_async_remote_copy(
        src_ref=expo, dst_ref=expo_x, send_sem=expo_sem.at[0], recv_sem=expo_sem.at[1],
        device_id=across, device_id_type=MESH)
    give_expo.start()

    sub = lax.broadcasted_iota(jnp.int32, (16, 128), 0) % 2 == 0
    first_lanes = lax.broadcasted_iota(jnp.int32, (16, 128), 1) < HALVES

    def arrange(k, raw):
        turned = pltpu.roll(raw, HALVES, 1)
        even = jnp.where(first_lanes, raw, pltpu.roll(turned, 15, 0))
        odd = jnp.where(first_lanes, pltpu.roll(turned, 1, 0), raw)
        table[k] = jnp.where(sub, even, odd).astype(F32) * 0.25

    arrange(0, expo[...])
    get_partners.wait()
    own_row = lax.broadcasted_iota(jnp.int32, (6, 128), 0) * 128 + lax.broadcasted_iota(jnp.int32, (6, 128), 1)
    local = jnp.where(ref < 8, own_row, partners[...] - ((ref + 8) % 16) * R).astype(F32)
    lane = lax.broadcasted_iota(jnp.int32, (128, 128), 1)
    line = lax.broadcasted_iota(jnp.int32, (128, 128), 0).astype(F32)
    for i in range(R // 128):
        row = jnp.broadcast_to(local[i:i + 1, :], (128, 128))
        column = jnp.transpose(row)
        for j in range(R // 128):
            turn[j * 128:(j + 1) * 128, i * 128:(i + 1) * 128] = (row == line + j * 128.0).astype(F32).astype(BF16)
            place = lane + j * 128
            stands = place
            for rows in ORDERED:
                stands = jnp.where(place >= PLACE[rows.start], place - PLACE[rows.start] + rows.start, stands)
            pick[i * 128:(i + 1) * 128, j * 128:(j + 1) * 128] = (column == stands.astype(F32)).astype(F32).astype(BF16)

    put_pick = fetch(pick.at[:, 0:LATE], pick_late)
    get_refs.wait()

    @pl.loop(0, K // W)
    def _(j):
        cols = pl.ds(pl.multiple_of(j * W, W), W)
        refs[:, cols] = jnp.dot(turn[...], raw[:, cols], preferred_element_type=F32).astype(BF16)

    @pl.loop(0, R // 128)
    def _(i):
        block = refs[pl.ds(i * 128, 128), :].astype(F32)
        total = jnp.sum(block * block, axis=1, keepdims=True)
        norms[pl.ds(i * 128, 128), :] = jnp.broadcast_to(total * (0.5 / K), (128, UNIT))

    def product(rows, unit, columns):
        return lax.dot_general(refs[rows, columns], img[unit * UNIT:(unit + 1) * UNIT, columns],
                               (((1,), (1,)), ((), ())), preferred_element_type=F32)

    def scores(unit, column=0, begun=False):
        bias = jnp.concatenate([
            table[dx, pl.ds((((y + dy + 4) % 4) * 2 + (h if dx == 0 else 1 - h)) * 2 + half, 1), :]
            for dx, dy, half in UNITS[unit]], axis=1)

        @pl.loop(0, 2)
        def _(i):
            r = pl.ds(pl.multiple_of(i * (R // 2), R // 2), R // 2)
            if begun:
                s = early[r, :] + product(r, unit, a_cols)
            else:
                s = product(r, unit, whole)
            wts[r, column:column + UNIT] = jnp.exp(s * (1.0 / 64.0) - norms[r, :] - bias).astype(BF16)

    def column_of(dl, dz):
        return pl.ds(pl.multiple_of((((l + dl) % 2) * 4 + (z + dz) % 4) * W, W), W)

    def accumulate(unit, units=1, start=False, bounds=(0, 8)):
        count = units * UNIT

        @pl.loop(*bounds)
        def _(j):
            added = jnp.dot(wts[:, 0:count], img[unit * UNIT:unit * UNIT + count, column_of(j // 4, j % 4)],
                            preferred_element_type=F32)
            acc[j] = added if start else acc[j] + added

    for copy in get_own:
        copy.wait()
    arrived("s0")
    scores(0)
    accumulate(0, start=True)

    arrived("own_0")
    share("s1", UNITS[1])
    send("far_b", part(0, -1, 0, b_cols), part(0, 2, 0, b_cols), up)
    send("far_b", part(0, 1, 1, b_cols), part(0, 2, 1, b_cols), down)
    send("x_5", part(0, -1, 0, b_cols), part(1, -1, 0, b_cols), across)
    send("x_5", part(0, 1, 1, b_cols), part(1, 1, 1, b_cols), across)
    send("far_a", part(0, -1, 0, a_cols), part(0, 2, 0, a_cols), up)
    send("far_a", part(0, 1, 1, a_cols), part(0, 2, 1, a_cols), down)
    arrived("s1")
    scores(1)
    accumulate(1)

    arrived("own_1")
    send("x_6", part(0, -1, 1, b_cols), part(1, -1, 1, b_cols), across)
    send("x_6", part(0, 1, 0, b_cols), part(1, 1, 0, b_cols), across)
    for k in range(2):
        send(f"y_{5 + k}", part(1, 0, k, a_cols), part(1, -1, k, a_cols), up)
        send(f"y_{5 + k}", part(1, 0, 1 - k, a_cols), part(1, 1, 1 - k, a_cols), down)
    share("s2", UNITS[2])
    share("s3", UNITS[3])
    give_expo.wait()
    arrange(1, expo_x[...])

    arrived("s2")
    scores(2)
    arrived("s3")
    scores(3, UNIT)
    accumulate(2, 2, bounds=(0, 4))
    arrived("far_b")
    quarter = HALVES // 2
    for k in range(4):
        at = (k // 2, b_cols, k % 2 * quarter, quarter)
        send("x_70" if k < 3 else "x_71", part(0, 2, *at), part(1, 2, *at), across)
    share("s4", UNITS[4], b_cols)
    arrived("x_5")
    share("s5", UNITS[5], b_cols)
    accumulate(2, 2, bounds=(4, 6))

    arrived("far_a")
    share("s4", UNITS[4], a_cols)
    accumulate(2, 2, bounds=(6, 8))
    arrived("s4")
    scores(4)
    accumulate(4, bounds=(0, 4))
    arrived("y_5")
    for k in range(2):
        at = (a_cols, k * quarter, quarter)
        send(f"y_7{k}", part(1, -1, 0, *at), part(1, 2, 0, *at), up)
        send(f"y_7{k}", part(1, 1, 1, *at), part(1, 2, 1, *at), down)
    share("s5", UNITS[5], a_cols)
    accumulate(4, bounds=(4, 8))
    arrived("s5")
    scores(5)
    arrived("x_6")
    share("s6b", UNITS[6], b_cols)
    accumulate(5, bounds=(0, 4))
    arrived("s6b")

    @pl.loop(0, 2)
    def _(i):
        r = pl.ds(pl.multiple_of(i * (R // 2), R // 2), R // 2)
        early[r, :] = product(r, 6, b_cols)

    arrived("y_6")
    share("s6a", UNITS[6], a_cols)
    accumulate(5, bounds=(4, 8))
    arrived("s6a")
    scores(6, begun=True)
    accumulate(6, bounds=(0, 4))
    arrived("y_70")
    share("s7", UNITS[7], a_cols, 0, quarter)
    arrived("x_70")
    share("s7", UNITS[7], b_cols, 0, quarter)
    share("s7", UNITS[7][:1], b_cols, quarter, quarter)
    accumulate(6, bounds=(4, 6))
    arrived("x_71")
    share("s7", UNITS[7][1:], b_cols, quarter, quarter)
    arrived("y_71")
    share("s7", UNITS[7], a_cols, quarter, quarter)
    accumulate(6, bounds=(6, 8))
    arrived("s7")
    scores(7)

    lo, hi = slice(0, HALF), slice(HALF, W)
    AB = slice(0, EARLY_ROWS.start), slice(EARLY_ROWS.stop, R)
    near = [slice(b.start - RA, b.stop - RA) for b in B_ROWS]

    def st_a(t, half, dl, a):
        return refs.at[a, pl.ds(pl.multiple_of(t * 1024 + half * W + dl * HALF, HALF), HALF)]

    def pair(t, half, a):
        return refs.at[a, t * 1024 + half * W:t * 1024 + half * W + W]

    def st_a2(k, a):
        return refs.at[a, 3072 + k * W:3072 + (k + 1) * W]

    def st_b(first, count, b):
        return refs.at[b, first:first + count]

    def a1(s):
        a = A_ROWS[s]
        send(f"a1{s}", pair(0, 0, a), r_a1.at[0, a, :], above)
        send(f"a1{s}", pair(0, 1, a), r_a1.at[1, a, :], below)

    def a2(s, up=True, down=True):
        if up:
            send(f"a2{s}", pair(1, 1, A_ROWS[s]), r_a2.at[0, A_ROWS[s], W:2 * W], above)
        if down:
            send(f"a2{s}", pair(2, 0, A_ROWS[s]), r_a2.at[1, A_ROWS[s], 0:W], below)

    def a2d(s):
        a = A_ROWS[s]
        arrived(f"a1{s}")
        for k, dz, cols, who in ((0, 1, lo, above), (1, 3, hi, below)):
            for dl in (1, 0):
                there = slice(dl * HALF, (dl + 1) * HALF)
                value = (acc[dl * 4 + dz, a, cols] + r_a1[k, a, there].astype(F32)).astype(BF16)
                refs[a, 3072 + k * W + dl * HALF:3072 + k * W + (dl + 1) * HALF] = value
            send(f"a2{s}", st_a2(k, a), r_a2.at[k, a, k * W:(k + 1) * W], who)

    def a3(s):
        a = A_ROWS[s]
        arrived(f"a2{s}")
        for dl in (1, 0):
            for half, cols in enumerate((lo, hi)):
                there = slice(half * W + dl * HALF, half * W + (dl + 1) * HALF)
                value = acc[dl * 4, a, cols] + r_a2[0, a, there].astype(F32) + r_a2[1, a, there].astype(F32)
                if dl:
                    wts[a, UNIT + half * HALF:UNIT + (half + 1) * HALF] = value.astype(BF16)
                else:
                    acc[0, a, cols] = value
            if dl:
                send(f"a3_{s}", wts.at[a, UNIT:UNIT + W], r_a3.at[a, :], beside)

    def b1(s, t):
        send(f"b1_{t}{s}" if t < 3 else f"b3{s}", st_b(t * W, W, B_ROWS[s]), r_b1.at[t, near[s], :], beside)

    def b2(s):
        b, n = B_ROWS[s], near[s]
        arrived(f"b1_0{s}")
        refs[b, 2048:2048 + W] = (acc[2, b, :] + r_b1[0, n, :].astype(F32)).astype(BF16)
        send(f"b2{s}", st_b(2048, HALF, b), r_b2.at[0, n, :], above)
        send(f"b2{s}", st_b(2048 + HALF, HALF, b), r_b2.at[1, n, :], below)

    def b3(s, k):
        b, n = B_ROWS[s], near[s]
        t, dz, cols, who = ((1, 1, hi, above), (2, 3, lo, below))[k]
        arrived(f"b1_{t}{s}")
        first = 2560 + k * HALF
        refs[b, first:first + HALF] = (acc[dz, b, cols] + r_b1[t, n, cols].astype(F32)).astype(BF16)
        send(f"b3{s}", st_b(first, HALF, b), r_b3.at[k, n, cols], who)

    def b3d(s):
        b, n = B_ROWS[s], near[s]
        arrived(f"b2{s}")
        for k, t, dz, cols, who in ((0, 1, 1, lo, above), (1, 2, 3, hi, below)):
            value = acc[dz, b, cols] + r_b1[t, n, cols].astype(F32) + r_b2[k, n, :].astype(F32)
            first = 3072 + k * HALF
            refs[b, first:first + HALF] = value.astype(BF16)
            send(f"b3{s}", st_b(first, HALF, b), r_b3.at[k, n, cols], who)

    def finish(name, rows):
        if name.endswith(str(LAST)):
            return
        final[rows, :] = acc[0, rows, :].astype(BF16)
        send(f"p1_{name}", final.at[rows, lo], relay.at[0, rows, :], up)
        send(f"p1_{name}", final.at[rows, hi], relay.at[1, rows, :], down)

    def finish_a(s):
        a = A_ROWS[s]
        arrived(f"a3_{s}")
        acc[0, a, :] = acc[0, a, :] + r_a3[a, :].astype(F32)
        finish(f"a{s}", a)

    def finish_b(s):
        b, n = B_ROWS[s], near[s]
        arrived(f"b3{s}")
        acc[0, b, :] = (acc[0, b, :] + r_b1[3, n, :].astype(F32)) + (r_b3[0, n, :].astype(F32) + r_b3[1, n, :].astype(F32))
        finish(f"b{s}", b)

    def pass_on(name, rows, s):
        arrived(f"p1_{name}")
        send(f"p2_{s}", relay.at[0, rows, :], other.at[rows, lo], up)
        send(f"p2_{s}", relay.at[1, rows, :], other.at[rows, hi], down)

    def settle(s):
        arrived(f"p2_{s}")
        for rows in (A_ROWS[s], B_ROWS[s]):
            value = acc[0, rows, :] + other[rows, :].astype(F32)
            at = slice(PLACE[rows.start], PLACE[rows.start] + rows.stop - rows.start)
            high[at, :] = value.astype(BF16)
            rest[at, :] = (value - value.astype(BF16).astype(F32)).astype(BF16)

    cuts = (0, R // 2, R * 5 // 6, R)

    def order(s, k):
        r = slice(k * (R // 2), (k + 1) * (R // 2)) if s == 0 else slice(cuts[k], cuts[k + 1])
        at = slice(PLACE[A_ROWS[s].start], PLACE[B_ROWS[s].start] + B_ROWS[s].stop - B_ROWS[s].start)
        value = jnp.dot(pick[r, at], high[at, :], preferred_element_type=F32)
        value = value + jnp.dot(pick[r, at], rest[at, :], preferred_element_type=F32)
        acc[6, r, :] = value if s == 0 else acc[6, r, :] + value

    def c2(t):
        arrived(f"c1_{t}")
        send("c2", c_pass.at[t, 0], c_in.at[t, 0], up)
        send("c2", c_pass.at[t, 1], c_in.at[t, 1], down)

    def cin():
        arrived("c2")
        a, b = A_ROWS[LAST], B_ROWS[LAST]
        split = a.stop - a.start
        for t, dz in enumerate(ORDER):
            for dl in range(2):
                value = acc[dl * 4 + dz, EARLY_ROWS, :] + c_in[t, dl].astype(F32)
                acc[dl * 4 + dz, EARLY_ROWS, :] = value
                if t < 3:
                    for half, cols in enumerate((lo, hi)):
                        first = t * 1024 + half * W + dl * HALF
                        refs[a, first:first + HALF] = value[:split, cols].astype(BF16)
                if dl == 1:
                    refs[b, t * W:(t + 1) * W] = value[split:].astype(BF16)

    def last_unit(t, dl):
        dz = ORDER[t]
        added = jnp.dot(wts[:, 0:UNIT], img[7 * UNIT:8 * UNIT, column_of(dl, dz)], preferred_element_type=F32)
        value = acc[dl * 4 + dz] + added
        acc[dl * 4 + dz] = value
        c_out[t, dl] = value[EARLY_ROWS].astype(BF16)
        if t < 3:
            for half, cols in enumerate((lo, hi)):
                st_a(t, half, dl, AB[0])[...] = value[AB[0], cols].astype(BF16)
        return value

    for dl in (1, 0):
        value = last_unit(0, dl)
        if dl == 1:
            refs[AB[1], 0:W] = value[AB[1]].astype(BF16)
            b1(0, 0)
        a = A_ROWS[0]
        for half, who in ((0, above), (1, below)):
            first = half * W + dl * HALF
            send("a10", refs.at[a, first:first + HALF], r_a1.at[half, a, dl * HALF:(dl + 1) * HALF], who)
        send("c1_0", c_out.at[0, dl], c_pass.at[0, dl], down if dl else up)

    for t in range(1, 4):
        @pl.loop(0, 2)
        def _(i):
            dl = 1 - i
            value = last_unit(t, dl)

            @pl.when(dl == 1)
            def _():
                refs[AB[1], t * W:(t + 1) * W] = value[AB[1]].astype(BF16)

        b1(0, t)
        if t == 1:
            a2(0, down=False)
        if t == 2:
            a2(0, up=False)
        send(f"c1_{t}", c_out.at[t, 0], c_pass.at[t, 0], up)
        send(f"c1_{t}", c_out.at[t, 1], c_pass.at[t, 1], down)

    puts = []

    def give(k):
        r = slice(cuts[k], cuts[k + 1])
        return fetch(acc.at[6, r, :], sums.at[r, :])

    a2d(0)
    c2(0)
    b1(1, 1)
    b1(1, 0)
    c2(3)
    c2(2)
    b2(0)
    a1(1)
    a3(0)
    b1(1, 2)
    b3(0, 1)
    c2(1)
    b3(0, 0)
    b3d(0)
    b2(1)
    a2(1)
    a2d(1)
    cin()
    b1(2, 0)
    b1(1, 3)
    finish_b(0)
    finish_a(0)
    b3(1, 0)
    b3(1, 1)
    b3d(1)
    pass_on("b0", B_ROWS[0], 0)
    a3(1)
    b1(2, 1)
    b1(2, 2)
    a1(2)
    b2(2)
    pass_on("a0", A_ROWS[0], 0)
    a2(2)
    finish_b(1)
    a2d(2)
    finish_a(1)
    b1(2, 3)
    settle(0)
    pass_on("b1", B_ROWS[1], 1)
    order(0, 1)
    b3(2, 1)
    b3(2, 0)
    a3(2)
    pass_on("a1", A_ROWS[1], 1)
    b3d(2)
    order(0, 0)
    finish_b(2)
    finish_a(2)
    puts.append(fetch(acc.at[0, EARLY_ROWS, :], late))
    settle(1)
    order(1, 0)
    puts.append(give(0))
    order(1, 1)
    puts.append(give(1))
    order(1, 2)
    puts.append(give(2))
    for copy in copies[-FLIGHT:]:
        copy.wait_send()
    for copy in [put_pick] + puts:
        copy.wait()


PARTS = 4


def average(pick_hbm, late_hbm, sums_hbm, out_hbm, pick, late, sums, out, in_sem, out_sem):
    rows = [slice(i * (R // PARTS), (i + 1) * (R // PARTS)) for i in range(PARTS)]
    fetches = [pltpu.make_async_copy(late_hbm, late, in_sem.at[PARTS]),
               pltpu.make_async_copy(pick_hbm, pick, in_sem.at[PARTS + 1])]
    fetches += [pltpu.make_async_copy(sums_hbm.at[r, :], sums.at[r, :], in_sem.at[i]) for i, r in enumerate(rows)]
    for copy in fetches:
        copy.start()
    fetches[0].wait()
    fetches[1].wait()
    high = late[...].astype(BF16)
    rest = (late[...] - high.astype(F32)).astype(BF16)
    puts = []
    for i, r in enumerate(rows):
        added = jnp.dot(pick[r, :], high, preferred_element_type=F32) + jnp.dot(pick[r, :], rest, preferred_element_type=F32)
        fetches[2 + i].wait()
        out[r, :] = (sums[r, :] + added) * (0.5 / 128.0)
        puts.append(pltpu.make_async_copy(out.at[r, :], out_hbm.at[r, :], out_sem.at[i]))
        puts[-1].start()
    for copy in puts:
        copy.wait()


VMEM = 67043328


def body(images, exponents, references, partners):
    anywhere = pl.BlockSpec(memory_space=pl.ANY)
    sums, late, pick = pl.pallas_call(
        kernel,
        out_shape=(jax.ShapeDtypeStruct((R, W), F32), jax.ShapeDtypeStruct((LATE, W), F32),
                   jax.ShapeDtypeStruct((R, LATE), BF16)),
        in_specs=[anywhere] * 4,
        out_specs=(anywhere,) * 3,
        scratch_shapes=[
            pltpu.VMEM((8 * UNIT, K), BF16),
            pltpu.VMEM((R, K), BF16),
            pltpu.VMEM((R, K), BF16),
            pltpu.VMEM((8, R, W), F32),
            pltpu.VMEM((R, 3 * UNIT), BF16),
            pltpu.VMEM((R, UNIT), F32),
            pltpu.VMEM((R, R), BF16),
            pltpu.VMEM((R, R), BF16),
            pltpu.VMEM((16, 128), jnp.int32),
            pltpu.VMEM((16, 128), jnp.int32),
            pltpu.VMEM((2, 16, 128), F32),
            pltpu.VMEM((6, 128), jnp.int32),
            pltpu.VMEM((R, UNIT), F32),
            pltpu.VMEM((2, RA, W), BF16),
            pltpu.VMEM((2, RA, 2 * W), BF16),
            pltpu.VMEM((RA, W), BF16),
            pltpu.VMEM((4, RB, W), BF16),
            pltpu.VMEM((2, RB, HALF), BF16),
            pltpu.VMEM((2, RB, W), BF16),
            pltpu.VMEM((4, 2, LATE, W), BF16),
            pltpu.VMEM((4, 2, LATE, W), BF16),
            pltpu.VMEM((4, 2, LATE, W), BF16),
            pltpu.VMEM((R, W), BF16),
            pltpu.VMEM((2, R, HALF), BF16),
            pltpu.VMEM((R, W), BF16),
            pltpu.VMEM((R, W), BF16),
            pltpu.VMEM((R, W), BF16),
            pltpu.SemaphoreType.DMA((10,)),
            pltpu.SemaphoreType.DMA((FLIGHT,)),
            pltpu.SemaphoreType.DMA((GROUPS,)),
            pltpu.SemaphoreType.DMA((2,)),
        ],
        compiler_params=pltpu.CompilerParams(
            collective_id=0, has_side_effects=True, vmem_limit_bytes=VMEM),
    )(images, exponents.reshape(16, 128), references, partners.reshape(6, 128))
    return pl.pallas_call(
        average,
        out_shape=jax.ShapeDtypeStruct((R, W), F32),
        in_specs=[anywhere] * 3,
        out_specs=anywhere,
        scratch_shapes=[
            pltpu.VMEM((R, LATE), BF16),
            pltpu.VMEM((LATE, W), F32),
            pltpu.VMEM((R, W), F32),
            pltpu.VMEM((R, W), F32),
            pltpu.SemaphoreType.DMA((PARTS + 2,)),
            pltpu.SemaphoreType.DMA((PARTS,)),
        ],
        compiler_params=pltpu.CompilerParams(vmem_limit_bytes=67043328),
    )(pick, late, sums)


def solution(mesh):
    in_specs = (P(("img", "ref"), None), P("img"), P("ref", None), P("ref"))
    out_specs = P("ref", "img")
    return jax.shard_map(body, mesh=mesh, in_specs=in_specs, out_specs=out_specs, check_vma=False)
```
